1024 devices in a mesh: wide: 32 (over x_hi, z), sec: 8 (over y), tile: 4 (over x_lo, core).
Axes of the slice: x: 8 (x_hi: 4, x_lo: 2; x = x_hi * 2 + x_lo), y: 8, z: 8, core: 2. Of those that a mesh axis runs over, the one named last changes fastest.
Arguments:
- velocity: float32 [3, 128, 64, 1024], P(None, 'wide', 'tile', 'sec'), may hold values from -0.4 to 0.4
- viscosity: float32 [128, 64, 1024], P('wide', 'tile', 'sec'), may hold values from 0.01 to 0.08
- counts: int32 [32, 8, 4], P('wide', 'sec', 'tile'), may hold values from 2 to 4, as said below
- destination: int32 [32, 8, 4, 4], P('wide', 'sec', 'tile'), may hold values from 0 to 3, as said below
- seeds: int32 [32, 8, 4, 4, 3, 128], P('wide', 'sec', 'tile'), may hold values from 0 to 127, as said below
- substeps: int32 [32, 8, 4, 4, 128], P('wide', 'sec', 'tile'), may hold values from 0 to 1
Outputs:
- new_velocity: float32 [3, 128, 64, 1024], P(None, 'wide', 'tile', 'sec')
- traced_blocks: float32 [32, 8, 4, 8, 3, 128], P('wide', 'sec', 'tile')
The draws below stay inside these ranges and needn't reach their ends.
Inputs may be any that keep to these rules, and one draw needn't show every extreme that they name: Blocks 0 to counts - 1 of a device are live; some device has all 4 live. `destination`: among a device's live blocks at most 2 name any one tile, and exactly 2 name the tile that all devices with the same wide and sec index share. `seeds`: components 0, 1, 2 lie below 4, 16, 128.
All inputs are finite; a program needn't handle non-finite values.
Results may differ from the reference program's by a relative error of at most 0.0003.
Values sent between devices are 32-bit elements; how exact they have to be, the bound alone decides.
No kernel may reach another device: no remote copies, remote signals or barrier semaphores. Data moves between devices by JAX's collectives and lax.ppermute only.
A program may use at most 64 MiB of HBM per device.

```python
import math
from functools import partial
import jax
import jax.numpy as jnp

CX = 4
CY = 16
CZ = 128
CAP = 2
PTS = 128
MAXSUB = 1
BLK_DEV = 4
SLOTS = 8
NX = 128
NY = 64
NZ = 1024
N_WIDE = 32
N_SEC = 8
N_TILE = 4


def routing_table(key):
    key = jax.random.fold_in(key, 11)
    keys = jax.random.split(key, 6)
    shape = (N_WIDE, N_SEC, N_TILE)
    counts = jax.random.randint(keys[0], shape, CAP, BLK_DEV + 1)
    chosen = jax.random.randint(keys[1], (), 0, N_WIDE * N_SEC * N_TILE)
    flat_ids = jnp.arange(N_WIDE * N_SEC * N_TILE, dtype=jnp.int32).reshape(shape)
    counts = jnp.where(flat_ids == chosen, BLK_DEV, counts).astype(jnp.int32)
    hottest = jax.random.randint(keys[2], (N_WIDE, N_SEC, 1, 1), 0, N_TILE)
    block_ids = jnp.arange(BLK_DEV, dtype=jnp.int32)
    others = jnp.mod(hottest + 1 + jax.random.randint(keys[3], shape + (BLK_DEV,), 0, N_TILE - 1), N_TILE)
    filler = jax.random.randint(keys[4], shape + (BLK_DEV,), 0, N_TILE)
    counted = counts[..., None]
    ranked = jnp.where(block_ids < CAP, hottest, jnp.where(block_ids < counted, others, filler))
    scores = jax.random.randint(keys[5], shape + (BLK_DEV,), 0, 1 << 20) * BLK_DEV + block_ids
    scores = jnp.where(block_ids < counted, scores, (1 << 26) + block_ids)
    permuted = jnp.argsort(scores, axis=-1, stable=True)
    chosen_dest = jnp.take_along_axis(ranked, permuted, -1).astype(jnp.int32)
    return (counts, chosen_dest)


def draw_counts(key, part):
    return routing_table(key)[0]


def draw_destination(key, part):
    return routing_table(key)[1]


def draw_seeds(key, part):
    key = jax.random.fold_in(key, 23)
    upper_bound = jnp.array([CX, CY, CZ], jnp.int32).reshape(3, 1)
    return jax.random.randint(key, (N_WIDE, N_SEC, N_TILE, BLK_DEV, 3, PTS), 0, upper_bound).astype(jnp.int32)


def set_ends(values, rng, least, high):
    shape = values.shape
    index_at = [jax.random.randint(jax.random.fold_in(rng, axis), (), 0, shape[axis]) for axis in range(len(shape))]
    values = values.at[tuple(index_at)].set(least)
    longest = shape.index(max(shape))
    index_at[longest] = (index_at[longest] + 1) % shape[longest]
    return values.at[tuple(index_at)].set(high)


def steps_of(own_key, extent, shards, least, largest):
    def one(dim, shards_of):
        draws = jax.random.uniform(jax.random.fold_in(jax.random.fold_in(own_key, 6), dim), (shards_of,), jnp.float32, least / len(shards), largest / len(shards))
        return jnp.repeat(jnp.exp(draws), extent[dim] // shards_of).reshape((-1,) + (1,) * (len(extent) - dim - 1))

    loudness = one(*shards[0])
    for cut in shards[1:]:
        loudness = loudness * one(*cut)
    return loudness


def setup_inputs(seed: int = 0) -> dict:
    streams_of = jax.random.split(jax.random.key(seed), 7)
    velocity = jnp.clip(jax.random.uniform(streams_of[0], (3, NX, NY, NZ), jnp.float32, -0.4, 0.4) * steps_of(streams_of[0], (3, NX, NY, NZ), ((1, 32), (2, 4), (3, 8)), -0.4, 0.0), -0.4, 0.4)
    viscosity = jnp.clip(jnp.exp(math.log(0.08) - 2.0794415 * jax.random.uniform(streams_of[1], (NX, NY, NZ), jnp.float32) ** steps_of(streams_of[1], (NX, NY, NZ), ((0, 32), (1, 4), (2, 8)), -0.2, 0.2)), 0.01, 0.08)
    counts = draw_counts(jax.random.fold_in(streams_of[6], 71), 0)
    destination = draw_destination(jax.random.fold_in(streams_of[6], 71), 0)
    seeds = draw_seeds(jax.random.fold_in(streams_of[6], 71), 0)
    substeps = set_ends(jax.random.randint(streams_of[5], (N_WIDE, N_SEC, N_TILE, BLK_DEV, PTS), 0, MAXSUB + 1), jax.random.fold_in(streams_of[5], 1), 0, MAXSUB).astype(jnp.int32)
    return {"velocity": velocity, "viscosity": viscosity, "counts": counts, "destination": destination, "seeds": seeds, "substeps": substeps}


flow_step = 0.2
trace_step = 1.25


def neighbor(padded, dimension, offset):
    window = [slice(None), slice(1, -1), slice(1, -1), slice(1, -1)]
    length = padded.shape[dimension]
    window[dimension] = slice(1 + offset, length - 1 + offset)
    return padded[tuple(window)]


def advance(padded, viscous):
    centre = padded[:, 1:-1, 1:-1, 1:-1]
    spread = jnp.zeros_like(centre)
    laplace = jnp.zeros_like(centre)
    for component in range(3):
        dimension = component + 1
        upper_cell = neighbor(padded, dimension, 1)
        lower_cell = neighbor(padded, dimension, -1)
        flux_up = 0.25 * (centre + upper_cell) * (centre[component] + upper_cell[component])
        flux_down = 0.25 * (lower_cell + centre) * (lower_cell[component] + centre[component])
        spread = spread + (flux_up - flux_down)
        laplace = laplace + (upper_cell + lower_cell)
    laplace = laplace - 6.0 * centre
    return centre + flow_step * (viscous * laplace - spread)


def runge_kutta(offset, sampler):
    section_one = sampler(offset)
    section_two = sampler(offset + (0.5 * trace_step) * section_one)
    section_three = sampler(offset + (0.5 * trace_step) * section_two)
    section_four = sampler(offset + trace_step * section_three)
    return offset + (trace_step / 6.0) * (section_one + 2.0 * section_two + 2.0 * section_three + section_four)


def march(offset, steps_float, sampler):
    for turn_index in range(MAXSUB):
        moved_off = runge_kutta(offset, sampler)
        offset = jnp.where(turn_index < steps_float, moved_off, offset)
    return offset


def global_sampler(flattened, cells, offset):
    lowest = jnp.floor(offset)
    fraction = offset - lowest
    corner = cells + lowest.astype(jnp.int32)
    summed = jnp.zeros_like(offset)
    for step_x in range(2):
        weight_x = fraction[0] if step_x else 1.0 - fraction[0]
        cell_x = jnp.mod(corner[0] + step_x, NX)
        for step_y in range(2):
            weight_y = fraction[1] if step_y else 1.0 - fraction[1]
            cell_y = corner[1] + step_y
            inside = (cell_y >= 0) & (cell_y < NY)
            clamped = jnp.clip(cell_y, 0, NY - 1)
            for step_z in range(2):
                weight_z = fraction[2] if step_z else 1.0 - fraction[2]
                cell_z = jnp.mod(corner[2] + step_z, NZ)
                linear = (cell_x * NY + clamped) * NZ + cell_z
                values = jnp.take(flattened, linear, axis=1)
                values = jnp.where(inside, values, 0.0)
                summed = summed + (weight_x * weight_y * weight_z) * values
    return summed


def reference(velocity, viscosity, counts, destination, seeds, substeps):
    padded = jnp.pad(velocity, ((0, 0), (1, 1), (0, 0), (1, 1)), mode="wrap")
    padded = jnp.pad(padded, ((0, 0), (0, 0), (1, 1), (0, 0)))
    fresh_vel = advance(padded, viscosity)
    flattened = fresh_vel.reshape(3, -1)
    wide_ids = jnp.broadcast_to(jnp.arange(N_WIDE, dtype=jnp.int32)[:, None, None, None], destination.shape)
    sec_ids = jnp.broadcast_to(jnp.arange(N_SEC, dtype=jnp.int32)[None, :, None, None], destination.shape)
    anchor = jnp.stack([wide_ids * CX, destination * CY, sec_ids * CZ], -1)
    start_cell = (seeds + anchor[..., None]).astype(jnp.int32)
    cells = jnp.moveaxis(start_cell, 4, 0).reshape(3, -1)
    steps_float = substeps.reshape(-1)
    offset = jnp.zeros(cells.shape, jnp.float32)
    traced = march(offset, steps_float, partial(global_sampler, flattened, cells))
    traced = jnp.moveaxis(traced.reshape(3, N_WIDE, N_SEC, N_TILE, BLK_DEV, PTS), 0, 4)
    tile_ids = jnp.arange(N_TILE, dtype=jnp.int32)
    block_ids = jnp.arange(BLK_DEV, dtype=jnp.int32)
    is_live = block_ids[None, None, None, :] < counts[..., None]
    onehot = ((destination[..., None] == tile_ids) & is_live[..., None]).astype(jnp.int32)
    order_rank = jnp.sum(onehot * (jnp.cumsum(onehot, 3) - onehot), -1)
    slot_index = tile_ids[None, None, :, None] * CAP + order_rank
    target = jnp.where(is_live, destination, N_TILE)
    result = jnp.zeros((N_WIDE, N_SEC, N_TILE, SLOTS, 3, PTS), jnp.float32)
    result = result.at[wide_ids, sec_ids, target, slot_index].set(traced, mode="drop")
    return fresh_vel, result
```

```python
from functools import partial

import jax
import jax.numpy as jnp
from jax import lax
from jax.experimental import pallas as pl
from jax.experimental.pallas import tpu as pltpu
from jax.sharding import PartitionSpec as P

CAP = 2
CX, CY, CZ = 4, 16, 128
TILES = 4
BLOCKS = 4
LX = CX + 4
LY = 24
N_VEL = 3 * LX
N_ALL = N_VEL + CX + 2
PER = CZ // 4
N_Z = -(-N_ALL * 3 // PER)
ROWS = 64
PT_ROW = 56

flow_step = 0.2
trace_step = 1.25

VMEM = pl.BlockSpec(memory_space=pltpu.VMEM)
SMEM = pl.BlockSpec(memory_space=pltpu.SMEM)


def plane_ref(group, vel, visc, xlo, xhi):
    if group < N_VEL:
        comp, x = divmod(group, LX)
        if x < 2:
            return xlo.at[2 * comp + x]
        if x < 2 + CX:
            return vel.at[comp, x - 2]
        return xhi.at[2 * comp + x - 2 - CX]
    x = group - N_VEL
    if x == 0:
        return xlo.at[6]
    if x <= CX:
        return visc.at[x - 1]
    return xhi.at[6]


def halo_rows(group):
    if group < N_VEL:
        return 2 * group, 2
    return 2 * N_VEL + group - N_VEL, 1


def y_kernel(counts, dest, seeds, substeps, vel, visc, xlo, xhi, out):
    tile = lax.axis_index("tile")
    live = [b < counts[0] for b in range(BLOCKS)]
    ranks = []
    for b in range(BLOCKS):
        rank = jnp.int32(0)
        for a in range(b):
            rank = rank + jnp.where(dest[a] == dest[b], 1, 0)
        ranks.append(rank)
    payload = [
        jnp.concatenate([seeds[b], substeps[b : b + 1, :]], 0).astype(jnp.float32)
        for b in range(BLOCKS)
    ]
    for d in range(TILES):
        for r in range(CAP):
            slot = jnp.zeros((4, CZ), jnp.float32)
            for b in range(BLOCKS):
                chosen = live[b] & (dest[b] == d) & (ranks[b] == r)
                slot = jnp.where(chosen, payload[b], slot)
            out[d, PT_ROW + 4 * r : PT_ROW + 4 * r + 4, :] = slot

    @pl.when(tile < TILES - 1)
    def _():
        for g in range(N_ALL):
            row, n = halo_rows(g)
            out[tile + 1, row : row + n, :] = plane_ref(g, vel, visc, xlo, xhi)[CY - n : CY, :]

    @pl.when(tile > 0)
    def _():
        for g in range(N_ALL):
            row, n = halo_rows(g)
            out[tile - 1, row : row + n, :] = plane_ref(g, vel, visc, xlo, xhi)[0:n, :]


def z_kernel(vel, visc, xlo, xhi, yrecv, whole, zmsg):
    tile = lax.axis_index("tile")
    below = jnp.maximum(tile - 1, 0)
    above = jnp.minimum(tile + 1, TILES - 1)
    lane = lax.broadcasted_iota(jnp.int32, (8, CZ), 1)
    packs = [jnp.zeros((8, CZ), jnp.float32) for _ in range(N_Z)]
    for g in range(N_ALL):
        row, n = halo_rows(g)
        plane = plane_ref(g, vel, visc, xlo, xhi)
        high = jnp.where(tile < TILES - 1, yrecv[above, row : row + n, :], 0.0)
        low = jnp.where(tile > 0, yrecv[below, row : row + n, :], 0.0)
        edge = jnp.concatenate([high, jnp.zeros((8 - 2 * n, CZ), jnp.float32), low], 0)
        parts = [plane[0:8, :], plane[8:16, :], edge]
        for i, part in enumerate(parts):
            whole[g, 8 * i : 8 * i + 8, :] = part
            v, k = divmod(3 * g + i, PER)
            moved = pltpu.roll(part, (4 * k + 2) % CZ, 1)
            packs[v] = jnp.where((lane >= 4 * k) & (lane < 4 * k + 4), moved, packs[v])
    for v in range(N_Z):
        zmsg[v] = packs[v]


def trace_kernel(whole, zlo, zhi, yrecv, fresh, traced, wide, near, table):
    tile = lax.axis_index("tile")
    lane = lax.broadcasted_iota(jnp.int32, (LY, CZ), 1)
    row = lax.broadcasted_iota(jnp.int32, (LY, CZ), 0)
    low_lane = lax.broadcasted_iota(jnp.int32, (8, CZ), 1) % 4 < 2
    merged = [jnp.where(low_lane, zlo[v], zhi[v]) for v in range(N_Z)]
    for g in range(N_ALL):
        for i in range(3):
            v, k = divmod(3 * g + i, PER)
            wide[g, 8 * i : 8 * i + 8, :] = pltpu.roll(merged[v], (CZ - 2 - 4 * k) % CZ, 1)

    def up_z(a, b):
        ra, rb = pltpu.roll(a, CZ - 1, 1), pltpu.roll(b, CZ - 1, 1)
        return jnp.where(lane < CZ - 1, ra, rb), jnp.where(lane < CZ - 1, rb, ra)

    def down_z(a, b):
        ra, rb = pltpu.roll(a, 1, 1), pltpu.roll(b, 1, 1)
        return jnp.where(lane > 0, ra, rb), jnp.where(lane > 0, rb, ra)

    outside = ((tile == 0) & (row == LY - 1)) | ((tile == TILES - 1) & (row == CY))

    def flux(one, two, d):
        both = one[d] + two[d]
        return [0.25 * (one[i] + two[i]) * both for i in range(3)]

    def new_plane(x):
        fields = []
        cells = [[r[i * LX + x + 1] for i in range(3)] for r in (whole, wide)]
        ups = [up_z(cells[0][i], cells[1][i]) for i in range(3)]
        downs = [down_z(cells[0][i], cells[1][i]) for i in range(3)]
        for half, src in enumerate((whole, wide)):
            c = cells[half]
            spread = [0.0] * 3
            laplace = [0.0] * 3
            for d in range(3):
                if d == 0:
                    upper = [src[i * LX + x + 2] for i in range(3)]
                    lower = [src[i * LX + x] for i in range(3)]
                elif d == 1:
                    upper = [pltpu.roll(c[i], LY - 1, 0) for i in range(3)]
                    lower = [pltpu.roll(c[i], 1, 0) for i in range(3)]
                else:
                    upper = [ups[i][half] for i in range(3)]
                    lower = [downs[i][half] for i in range(3)]
                f_up, f_down = flux(c, upper, d), flux(lower, c, d)
                spread = [spread[i] + (f_up[i] - f_down[i]) for i in range(3)]
                laplace = [laplace[i] + (upper[i] + lower[i]) for i in range(3)]
            viscous = src[N_VEL + x]
            fields.append(
                [
                    c[i] + flow_step * (viscous * (laplace[i] - 6.0 * c[i]) - spread[i])
                    for i in range(3)
                ]
            )
        for i in range(3):
            if 1 <= x <= CX:
                fresh[i, x - 1] = fields[0][i][:CY]
            a, b = (jnp.where(outside, 0.0, fields[h][i]) for h in range(2))
            for dz, field in enumerate((down_z(a, b)[0], a, up_z(a, b)[0])):
                near[x, i, 0, dz] = pltpu.roll(field, 1, 0)[:CY]
                near[x, i, 1, dz] = field[:CY]
                near[x, i, 2, dz] = pltpu.roll(field, LY - 1, 0)[:CY]

    for x in range(CX + 2):
        new_plane(x)

    def sample(x, e):
        weights = [(jnp.maximum(-v, 0.0), 1.0 - jnp.abs(v), jnp.maximum(v, 0.0)) for v in e]
        total = [0.0] * 3
        for dx in range(3):
            plane = [0.0] * 3
            for dy in range(3):
                for i in range(3):
                    line = sum(weights[2][dz] * near[x + dx, i, dy, dz] for dz in range(3))
                    plane[i] = plane[i] + weights[1][dy] * line
            total = [total[i] + weights[0][dx] * plane[i] for i in range(3)]
        return total

    for x in range(CX):
        k1 = [near[x + 1, i, 1, 1] for i in range(3)]
        k2 = sample(x, [(0.5 * trace_step) * v for v in k1])
        k3 = sample(x, [(0.5 * trace_step) * v for v in k2])
        k4 = sample(x, [trace_step * v for v in k3])
        for i in range(3):
            moved = (trace_step / 6.0) * (k1[i] + 2.0 * k2[i] + 2.0 * k3[i] + k4[i])
            first = i * CX * CY + x * CY
            rest = moved
            for part in range(3):
                piece = rest.astype(jnp.bfloat16)
                table[part * 3 * CX * CY + first : part * 3 * CX * CY + first + CY, :] = piece
                rest = rest - piece.astype(jnp.float32)

    zs = lax.broadcasted_iota(jnp.int32, (CZ, CZ), 0)
    xys = lax.broadcasted_iota(jnp.int32, (CX * CY, CZ), 0)
    for s in range(TILES):
        for r in range(CAP):
            point = yrecv[s, PT_ROW + 4 * r : PT_ROW + 4 * r + 4, :].astype(jnp.int32)
            pick = jnp.where(zs == point[2:3], 1.0, 0.0).astype(jnp.bfloat16)
            got = jnp.dot(table[...], pick, preferred_element_type=jnp.float32)
            size = 3 * CX * CY
            got = got[:size] + got[size : 2 * size] + got[2 * size :]
            here = (xys == point[0:1] * CY + point[1:2]) & (point[3:4] > 0)
            for i in range(3):
                value = jnp.where(here, got[i * CX * CY : (i + 1) * CX * CY], 0.0)
                traced[s * CAP + r, i : i + 1, :] = jnp.sum(value, 0, keepdims=True)


def shards(velocity, viscosity, counts, destination, seeds, substeps):
    def ring(axis):
        n = lax.axis_size(axis)
        forward = [(i, (i + 1) % n) for i in range(n)]
        return forward, [(b, a) for a, b in forward]

    f32 = jnp.float32
    to_high = jnp.concatenate([velocity[:, CX - 2 :].reshape(6, CY, CZ), viscosity[CX - 1 :]], 0)
    to_low = jnp.concatenate([velocity[:, :2].reshape(6, CY, CZ), viscosity[:1]], 0)
    forward, backward = ring("wide")
    xlo = lax.ppermute(to_high, "wide", forward)
    xhi = lax.ppermute(to_low, "wide", backward)
    ymsg = pl.pallas_call(
        y_kernel,
        out_shape=jax.ShapeDtypeStruct((TILES, ROWS, CZ), f32),
        in_specs=[SMEM, SMEM] + [VMEM] * 6,
        out_specs=VMEM,
        name="pack_y",
    )(
        counts.reshape(1),
        destination.reshape(BLOCKS),
        seeds.reshape(BLOCKS, 3, CZ),
        substeps.reshape(BLOCKS, CZ),
        velocity,
        viscosity,
        xlo,
        xhi,
    )
    yrecv = lax.all_to_all(ymsg, "tile", split_axis=0, concat_axis=0, tiled=True)
    whole, zmsg = pl.pallas_call(
        z_kernel,
        out_shape=(
            jax.ShapeDtypeStruct((N_ALL, LY, CZ), f32),
            jax.ShapeDtypeStruct((N_Z, 8, CZ), f32),
        ),
        in_specs=[VMEM] * 5,
        out_specs=(VMEM, VMEM),
        name="pack_z",
    )(velocity, viscosity, xlo, xhi, yrecv)
    forward, backward = ring("sec")
    zlo = lax.ppermute(zmsg, "sec", forward)
    zhi = lax.ppermute(zmsg, "sec", backward)
    fresh, traced = pl.pallas_call(
        trace_kernel,
        out_shape=(
            jax.ShapeDtypeStruct((3, CX, CY, CZ), f32),
            jax.ShapeDtypeStruct((TILES * CAP, 3, CZ), f32),
        ),
        in_specs=[VMEM] * 4,
        out_specs=(VMEM, VMEM),
        scratch_shapes=[
            pltpu.VMEM((N_ALL, LY, CZ), f32),
            pltpu.VMEM((CX + 2, 3, 3, 3, CY, CZ), f32),
            pltpu.VMEM((9 * CX * CY, CZ), jnp.bfloat16),
        ],
        name="trace",
    )(whole, zlo, zhi, yrecv)
    return fresh, traced[None, None, None]


def solution(mesh):
    in_specs = (
        P(None, "wide", "tile", "sec"),
        P("wide", "tile", "sec"),
        P("wide", "sec", "tile"),
        P("wide", "sec", "tile", None),
        P("wide", "sec", "tile", None, None, None),
        P("wide", "sec", "tile", None, None),
    )
    out_specs = (P(None, "wide", "tile", "sec"), P("wide", "sec", "tile", None, None, None))
    return jax.shard_map(shards, mesh=mesh, in_specs=in_specs, out_specs=out_specs, check_vma=False)
```

```python
from functools import partial

import jax
import jax.numpy as jnp
from jax import lax
from jax.experimental import pallas as pl
from jax.experimental.pallas import tpu as pltpu
from jax.sharding import PartitionSpec as P

CAP = 2
CX, CY, CZ = 4, 16, 128
TILES = 4
BLOCKS = 4
SLOTS = TILES * CAP
LX = CX + 4
LY = 24
N_VEL = 3 * LX
N_ALL = N_VEL + CX + 2
ROWS = 64
PT_ROW = 56
WIDTH = CZ // LX

flow_step = 0.2
trace_step = 1.25

VMEM = pl.BlockSpec(memory_space=pltpu.VMEM)
SMEM = pl.BlockSpec(memory_space=pltpu.SMEM)
f32 = jnp.float32


def call(kernel, name, out_shape, in_specs, scratch=(), flops=0, moved=0):
    return pl.pallas_call(
        kernel,
        out_shape=out_shape,
        in_specs=in_specs,
        out_specs=jax.tree.map(lambda _: VMEM, out_shape),
        scratch_shapes=list(scratch),
        compiler_params=pltpu.CompilerParams(vmem_limit_bytes=8 << 20),
        cost_estimate=pl.CostEstimate(flops=flops, bytes_accessed=moved, transcendentals=0),
        name=name,
    )


def shape(*dims):
    return jax.ShapeDtypeStruct(dims, f32)


def group_of(group):
    if group < N_VEL:
        return divmod(group, LX)
    return 3, group - N_VEL + 1


def plane_ref(group, vel, visc, xlo, xhi):
    comp, x = group_of(group)
    if x < 2:
        return xlo.at[2 * comp + x] if comp < 3 else xlo.at[6]
    if x < 2 + CX:
        return vel.at[comp, x - 2] if comp < 3 else visc.at[x - 2]
    return xhi.at[2 * comp + x - 2 - CX] if comp < 3 else xhi.at[6]


def inner(group):
    return 2 <= group_of(group)[1] < 2 + CX


def halo_rows(group):
    if group < N_VEL:
        return 2 * group, 2
    return 2 * N_VEL + group - N_VEL, 1


def x_kernel(vel, visc, to_high, to_low):
    for out, first, edge in ((to_high, CX - 2, CX - 1), (to_low, 0, 0)):
        for c in range(3):
            out[2 * c : 2 * c + 2] = vel[c, first : first + 2]
        out[6] = visc[edge]


def write_rows(groups, out, planes):
    tile = lax.axis_index("tile")

    @pl.when(tile < TILES - 1)
    def _():
        for g in groups:
            row, n = halo_rows(g)
            out[tile + 1, row : row + n, :] = planes(g)[CY - n : CY, :]

    @pl.when(tile > 0)
    def _():
        for g in groups:
            row, n = halo_rows(g)
            out[tile - 1, row : row + n, :] = planes(g)[0:n, :]


def points_kernel(counts, dest, seeds, substeps, vel, visc, out):
    live = [b < counts[0] for b in range(BLOCKS)]
    ranks = []
    for b in range(BLOCKS):
        rank = jnp.int32(0)
        for a in range(b):
            rank = rank + jnp.where(dest[a] == dest[b], 1, 0)
        ranks.append(rank)
    payload = [
        jnp.concatenate([seeds[c, b : b + 1, :] for c in range(3)] + [substeps[b : b + 1, :]], 0)
        for b in range(BLOCKS)
    ]
    for d in range(TILES):
        for r in range(CAP):
            slot = jnp.zeros((4, CZ), jnp.int32)
            for b in range(BLOCKS):
                chosen = live[b] & (dest[b] == d) & (ranks[b] == r)
                slot = jnp.where(chosen, payload[b], slot)
            out[d, PT_ROW + 4 * r : PT_ROW + 4 * r + 4, :] = slot.astype(f32)
    groups = [g for g in range(N_ALL) if inner(g)]
    write_rows(groups, out, lambda g: plane_ref(g, vel, visc, None, None))


def y_kernel(base, xlo, xhi, out):
    out[...] = base[...]
    groups = [g for g in range(N_ALL) if not inner(g)]
    write_rows(groups, out, lambda g: plane_ref(g, None, None, xlo, xhi))


def columns(part, group, lane, acc):
    comp, x = group_of(group)
    place = WIDTH * x + 4 * comp
    moved = pltpu.roll(part, (place + 2) % CZ, 1)
    return jnp.where((lane >= place) & (lane < place + 4), moved, acc)


def z_kernel(vel, visc, xlo, xhi, out):
    lane = lax.broadcasted_iota(jnp.int32, (CY, CZ), 1)
    acc = jnp.zeros((CY, CZ), f32)
    for g in range(N_ALL):
        acc = columns(plane_ref(g, vel, visc, xlo, xhi)[...], g, lane, acc)
    out[...] = acc


def edge_rows_kernel(yrecv, zpart, edges, zmsg):
    tile = lax.axis_index("tile")
    below = jnp.maximum(tile - 1, 0)
    above = jnp.minimum(tile + 1, TILES - 1)
    lane = lax.broadcasted_iota(jnp.int32, (8, CZ), 1)
    acc = jnp.zeros((8, CZ), f32)
    for g in range(N_ALL):
        row, n = halo_rows(g)
        high = jnp.where(tile < TILES - 1, yrecv[above, row : row + n, :], 0.0)
        low = jnp.where(tile > 0, yrecv[below, row : row + n, :], 0.0)
        edge = jnp.concatenate([high, jnp.zeros((8 - 2 * n, CZ), f32), low], 0)
        edges[g] = edge
        acc = columns(edge, g, lane, acc)
    zmsg[0:CY, :] = zpart[...]
    zmsg[CY:LY, :] = acc


def outside_walls():
    tile = lax.axis_index("tile")
    row = lax.broadcasted_iota(jnp.int32, (LY, CZ), 0)
    return ((tile == 0) & (row == LY - 1)) | ((tile == TILES - 1) & (row == CY))


def flux(one, two, d):
    both = one[d] + two[d]
    return [0.25 * (one[i] + two[i]) * both for i in range(3)]


def advance(c, viscous, sides):
    spread = [0.0] * 3
    laplace = [0.0] * 3
    for d, (lower, upper) in enumerate(sides):
        f_up, f_down = flux(c, upper, d), flux(lower, c, d)
        spread = [spread[i] + (f_up[i] - f_down[i]) for i in range(3)]
        laplace = [laplace[i] + (upper[i] + lower[i]) for i in range(3)]
    return [
        c[i] + flow_step * (viscous * (laplace[i] - 6.0 * c[i]) - spread[i]) for i in range(3)
    ]


def both_ways(fields, step, axis):
    n = fields[0].shape[axis]
    return (
        [pltpu.roll(v, step, axis) for v in fields],
        [pltpu.roll(v, n - step, axis) for v in fields],
    )


def runge_kutta(near):
    def sample(e):
        weights = [(jnp.maximum(-v, 0.0), 1.0 - jnp.abs(v), jnp.maximum(v, 0.0)) for v in e]
        total = [0.0] * 3
        for dx in range(3):
            plane = [0.0] * 3
            for dy in range(3):
                for i in range(3):
                    line = sum(weights[2][dz] * near(i, dx, dy, dz) for dz in range(3))
                    plane[i] = plane[i] + weights[1][dy] * line
            total = [total[i] + weights[0][dx] * plane[i] for i in range(3)]
        return total

    k1 = [near(i, 1, 1, 1) for i in range(3)]
    k2 = sample([(0.5 * trace_step) * v for v in k1])
    k3 = sample([(0.5 * trace_step) * v for v in k2])
    k4 = sample([trace_step * v for v in k3])
    return [
        (trace_step / 6.0) * (k1[i] + 2.0 * k2[i] + 2.0 * k3[i] + k4[i]) for i in range(3)
    ]


def points_of(yrecv, slot):
    s, r = divmod(slot, CAP)
    rows = yrecv[s, PT_ROW + 4 * r : PT_ROW + 4 * r + 4, :].astype(jnp.int32)
    return [rows[k : k + 1] for k in range(4)]


def at_edge(z):
    return (z < 2) | (z >= CZ - 2)


def lanes_of(table, index):
    return jnp.take_along_axis(table, index, axis=1, mode="promise_in_bounds")


def main_kernel(vel, visc, xlo, xhi, edges, yrecv, fresh, traced, strip, whole, near, table):
    lane = lax.broadcasted_iota(jnp.int32, (LY, CZ), 1)
    strips = [jnp.zeros((LY, CZ), f32) for _ in range(4)]
    for g in range(N_ALL):
        comp, x = group_of(g)
        whole[g, 0:CY, :] = plane_ref(g, vel, visc, xlo, xhi)[...]
        whole[g, CY:LY, :] = edges[g]
        plane = whole[g]
        place = WIDTH * x
        early = pltpu.roll(plane, (place + 2) % CZ, 1)
        late = pltpu.roll(plane, (place + 12) % CZ, 1)
        acc = jnp.where((lane >= place + 2) & (lane < place + 6), early, strips[comp])
        strips[comp] = jnp.where((lane >= place + 8) & (lane < place + 12), late, acc)
    for comp in range(4):
        strip[comp] = strips[comp]

    outside = outside_walls()
    for x in range(CX + 2):
        c = [whole[i * LX + x + 1] for i in range(3)]
        sides = [
            ([whole[i * LX + x] for i in range(3)], [whole[i * LX + x + 2] for i in range(3)]),
            both_ways(c, 1, 0),
            both_ways(c, 1, 1),
        ]
        new = advance(c, whole[N_VEL + x], sides)
        for i in range(3):
            if 1 <= x <= CX:
                fresh[i, x - 1] = new[i][:CY]
            a = jnp.where(outside, 0.0, new[i])
            for dz, field in enumerate((pltpu.roll(a, 1, 1), a, pltpu.roll(a, CZ - 1, 1))):
                near[x, i, 0, dz] = pltpu.roll(field, 1, 0)[:CY]
                near[x, i, 1, dz] = field[:CY]
                near[x, i, 2, dz] = pltpu.roll(field, LY - 1, 0)[:CY]

    for x in range(CX):
        moved = runge_kutta(lambda i, dx, dy, dz: near[x + dx, i, dy, dz])
        for i in range(3):
            table[i, x * CY : (x + 1) * CY, :] = moved[i]

    rows = lax.broadcasted_iota(jnp.int32, (CX * CY, CZ), 0)
    for slot in range(SLOTS):
        sx, sy, sz, steps = points_of(yrecv, slot)
        here = (rows == sx * CY + sy) & (steps > 0) & ~at_edge(sz)
        index = jnp.broadcast_to(sz, (8, CZ))
        for i in range(3):
            got = jnp.concatenate(
                [lanes_of(table[i, 8 * k : 8 * k + 8, :], index) for k in range(CX * CY // 8)], 0
            )
            traced[i, slot : slot + 1, :] = jnp.sum(jnp.where(here, got, 0.0), 0, keepdims=True)


def strip_kernel(strip, zlo, zhi, yrecv, fresh_in, traced_in, fresh, traced):
    lane = lax.broadcasted_iota(jnp.int32, (LY, CZ), 1)
    place = lane % WIDTH
    low, high = zlo[...], zhi[...]
    fields = []
    for comp in range(4):
        before = pltpu.roll(low, (CZ - 4 * comp) % CZ, 1)
        after = pltpu.roll(high, (CZ + 10 - 4 * comp) % CZ, 1)
        own = strip[comp]
        own = jnp.where(place < 2, before, own)
        fields.append(jnp.where((place == 12) | (place == 13), after, own))
    c = fields[:3]
    new = advance(c, fields[3], [both_ways(c, WIDTH, 1), both_ways(c, 1, 0), both_ways(c, 1, 1)])

    column = lax.broadcasted_iota(jnp.int32, (CY, CZ), 1)
    for i in range(3):
        part = new[i][:CY]
        for x in range(CX):
            first = WIDTH * (x + 2)
            left = pltpu.roll(part, (CZ - first - 2) % CZ, 1)
            right = pltpu.roll(part, (2 * CZ - 1 - first - 11) % CZ, 1)
            value = jnp.where(column == CZ - 1, right, fresh_in[i, x])
            fresh[i, x] = jnp.where(column == 0, left, value)

    outside = outside_walls()
    near = {}
    for i in range(3):
        a = jnp.where(outside, 0.0, new[i])
        for dz, field in enumerate((pltpu.roll(a, 1, 1), a, pltpu.roll(a, CZ - 1, 1))):
            shifts = (pltpu.roll(field, 1, 0), field, pltpu.roll(field, LY - 1, 0))
            for dy, shifted in enumerate(shifts):
                part = shifted[:CY]
                near[i, 0, dy, dz] = pltpu.roll(part, WIDTH, 1)
                near[i, 1, dy, dz] = part
                near[i, 2, dy, dz] = pltpu.roll(part, CZ - WIDTH, 1)
    moved = runge_kutta(lambda *key: near[key])

    rows = lax.broadcasted_iota(jnp.int32, (CY, CZ), 0)
    for slot in range(SLOTS):
        sx, sy, sz, steps = points_of(yrecv, slot)
        here = (rows == sy) & (steps > 0) & at_edge(sz)
        offset = jnp.where(sz < 2, sz + 2, sz - (CZ - 2) + 10)
        index = jnp.where(at_edge(sz), WIDTH * (sx + 2) + offset, 0)
        index = jnp.broadcast_to(index, (8, CZ))
        for i in range(3):
            got = jnp.concatenate([lanes_of(moved[i][8 * k : 8 * k + 8], index) for k in range(2)], 0)
            value = jnp.sum(jnp.where(here, got, 0.0), 0, keepdims=True)
            traced[i, slot : slot + 1, :] = traced_in[i, slot : slot + 1, :] + value


def shards(velocity, viscosity, counts, destination, seeds, substeps):
    def ring(axis):
        n = lax.axis_size(axis)
        forward = [(i, (i + 1) % n) for i in range(n)]
        return forward, [(b, a) for a, b in forward]

    message = shape(7, CY, CZ)
    to_high, to_low = call(x_kernel, "pack_x", (message, message), [VMEM] * 2)(velocity, viscosity)
    forward, backward = ring("wide")
    xlo = lax.ppermute(to_high, "wide", forward)
    xhi = lax.ppermute(to_low, "wide", backward)
    base = call(
        points_kernel,
        "points",
        shape(TILES, ROWS, CZ),
        [SMEM, SMEM] + [VMEM] * 4,
        flops=1 << 20,
        moved=1 << 20,
    )(
        counts.reshape(1),
        destination.reshape(BLOCKS),
        jnp.swapaxes(seeds.reshape(BLOCKS, 3, CZ), 0, 1),
        substeps.reshape(BLOCKS, CZ),
        velocity,
        viscosity,
    )
    ymsg = call(y_kernel, "pack_y", shape(TILES, ROWS, CZ), [VMEM] * 3)(base, xlo, xhi)
    yrecv = lax.all_to_all(ymsg, "tile", split_axis=0, concat_axis=0, tiled=True)
    zpart = call(z_kernel, "pack_z", shape(CY, CZ), [VMEM] * 4, flops=1 << 20, moved=1 << 20)(
        velocity, viscosity, xlo, xhi
    )
    edges, zmsg = call(
        edge_rows_kernel, "pack_edge", (shape(N_ALL, 8, CZ), shape(LY, CZ)), [VMEM] * 2
    )(yrecv, zpart)
    forward, backward = ring("sec")
    zlo = lax.ppermute(zmsg, "sec", forward)
    zhi = lax.ppermute(zmsg, "sec", backward)
    fresh, traced, strip = call(
        main_kernel,
        "trace",
        (shape(3, CX, CY, CZ), shape(3, SLOTS, CZ), shape(4, LY, CZ)),
        [VMEM] * 6,
        [
            pltpu.VMEM((N_ALL, LY, CZ), f32),
            pltpu.VMEM((CX + 2, 3, 3, 3, CY, CZ), f32),
            pltpu.VMEM((3, CX * CY, CZ), f32),
        ],
        flops=1 << 22,
        moved=1 << 23,
    )(velocity, viscosity, xlo, xhi, edges, yrecv)
    fresh, traced = call(
        strip_kernel,
        "strip",
        (shape(3, CX, CY, CZ), shape(3, SLOTS, CZ)),
        [VMEM] * 6,
    )(strip, zlo, zhi, yrecv, fresh, traced)
    return fresh, jnp.swapaxes(traced, 0, 1)[None, None, None]


def solution(mesh):
    in_specs = (
        P(None, "wide", "tile", "sec"),
        P("wide", "tile", "sec"),
        P("wide", "sec", "tile"),
        P("wide", "sec", "tile", None),
        P("wide", "sec", "tile", None, None, None),
        P("wide", "sec", "tile", None, None),
    )
    out_specs = (P(None, "wide", "tile", "sec"), P("wide", "sec", "tile", None, None, None))
    return jax.shard_map(shards, mesh=mesh, in_specs=in_specs, out_specs=out_specs, check_vma=False)
```

```python
import jax
import jax.numpy as jnp
from jax import lax
from jax.experimental import pallas as pl
from jax.experimental.pallas import tpu as pltpu
from jax.sharding import PartitionSpec as P


CAP = 2
CX, CY, CZ = 4, 16, 128
TILES = 4
BLOCKS = 4
SLOTS = TILES * CAP
LX = CX + 4
LY = 24
N_VEL = 3 * LX
N_ALL = N_VEL + CX + 2
HALO_ROWS = 26
PT_ROW = 56
ROWS = 64
WIDTH = CZ // LX

flow_step = 0.2
trace_step = 1.25

VMEM = pl.BlockSpec(memory_space=pltpu.VMEM)
SMEM = pl.BlockSpec(memory_space=pltpu.SMEM)
f32 = jnp.float32


def call(kernel, out_shape, in_specs, scratch=(), flops=0, moved=0):
    return pl.pallas_call(
        kernel,
        out_shape=out_shape,
        in_specs=in_specs,
        out_specs=jax.tree.map(lambda _: VMEM, out_shape),
        scratch_shapes=list(scratch),
        compiler_params=pltpu.CompilerParams(vmem_limit_bytes=8 << 20),
        cost_estimate=pl.CostEstimate(flops=flops, bytes_accessed=moved, transcendentals=0),
    )


def shape(*dims):
    return jax.ShapeDtypeStruct(dims, f32)


def group_of(group):
    if group < N_VEL:
        return divmod(group, LX)
    return 3, group - N_VEL + 1


def plane_ref(group, own, xlo, xhi):
    comp, x = group_of(group)
    if x < 2:
        return xlo.at[2 * comp + x] if comp < 3 else xlo.at[6]
    if x < 2 + CX:
        return own.at[CX * comp + x - 2]
    return xhi.at[2 * comp + x - 2 - CX] if comp < 3 else xhi.at[6]


def inner(group):
    return 2 <= group_of(group)[1] < 2 + CX


def halo_rows(group):
    kind = [g for g in range(N_ALL) if inner(g) == inner(group)]
    first = HALO_ROWS if inner(group) else 0
    vels = [g for g in kind if g < N_VEL]
    if group < N_VEL:
        return first + 2 * kind.index(group), 2
    return first + len(vels) + kind.index(group), 1


def next_tiles():
    tile = lax.axis_index("tile")
    return (tile + 1) % TILES, (tile + TILES - 1) % TILES


def write_x(own, message, first, edge):
    for c in range(3):
        message[2 * c : 2 * c + 2] = own[CX * c + first : CX * c + first + 2]
    message[6] = own[3 * CX + edge]


def prepare_kernel(counts, dest, seeds, substeps, own, to_high, to_low, out):
    write_x(own, to_high, CX - 2, CX - 1)
    write_x(own, to_low, 0, 0)
    live = [b < counts[0, 0, 0] for b in range(BLOCKS)]
    ranks = []
    for b in range(BLOCKS):
        rank = jnp.int32(0)
        for a in range(b):
            rank = rank + jnp.where(dest[a] == dest[b], 1, 0)
        ranks.append(rank)
    payload = [
        jnp.concatenate([seeds[c, b : b + 1, :] for c in range(3)] + [substeps[b : b + 1, :]], 0)
        for b in range(BLOCKS)
    ]
    for d in range(TILES):
        for r in range(CAP):
            slot = jnp.zeros((4, CZ), jnp.int32)
            for b in range(BLOCKS):
                chosen = live[b] & (dest[b] == d) & (ranks[b] == r)
                slot = jnp.where(chosen, payload[b], slot)
            out[d, PT_ROW + 4 * r : PT_ROW + 4 * r + 4, :] = slot.astype(f32)
    up, down = next_tiles()
    for g in range(N_ALL):
        if inner(g):
            row, n = halo_rows(g)
            plane = plane_ref(g, own, None, None)
            out[up, row : row + n, :] = plane[CY - n : CY, :]
            out[down, row : row + n, :] = plane[0:n, :]


def y_kernel(base, xlo, xhi, out):
    out[...] = base[...]
    up, down = next_tiles()
    for g in range(N_ALL):
        if not inner(g):
            row, n = halo_rows(g)
            plane = plane_ref(g, None, xlo, xhi)
            out[up, row : row + n, :] = plane[CY - n : CY, :]
            out[down, row : row + n, :] = plane[0:n, :]


def columns(part, group, lane, acc):
    comp, x = group_of(group)
    place = WIDTH * x + 4 * comp
    moved = pltpu.roll(part, (place + 2) % CZ, 1)
    return jnp.where((lane >= place) & (lane < place + 4), moved, acc)


def z_kernel(own, xlo, xhi, out):
    lane = lax.broadcasted_iota(jnp.int32, (CY, CZ), 1)
    acc = jnp.zeros((CY, CZ), f32)
    for g in range(N_ALL):
        acc = columns(plane_ref(g, own, xlo, xhi)[...], g, lane, acc)
    out[...] = acc


def edge_rows_kernel(yrecv, zpart, edges, zmsg):
    tile = lax.axis_index("tile")
    below = jnp.maximum(tile - 1, 0)
    above = jnp.minimum(tile + 1, TILES - 1)
    lane = lax.broadcasted_iota(jnp.int32, (8, CZ), 1)
    acc = jnp.zeros((8, CZ), f32)
    for g in range(N_ALL):
        row, n = halo_rows(g)
        high = jnp.where(tile < TILES - 1, yrecv[above, row : row + n, :], 0.0)
        low = jnp.where(tile > 0, yrecv[below, row : row + n, :], 0.0)
        edge = jnp.concatenate([high, jnp.zeros((8 - 2 * n, CZ), f32), low], 0)
        edges[g] = edge
        acc = columns(edge, g, lane, acc)
    zmsg[0:CY, :] = zpart[...]
    zmsg[CY:LY, :] = acc


def outside_walls():
    tile = lax.axis_index("tile")
    row = lax.broadcasted_iota(jnp.int32, (LY, CZ), 0)
    return ((tile == 0) & (row == LY - 1)) | ((tile == TILES - 1) & (row == CY))


def flux(one, two, d):
    both = one[d] + two[d]
    return [0.25 * (one[i] + two[i]) * both for i in range(3)]


def advance(c, viscous, sides):
    spread = [0.0] * 3
    laplace = [0.0] * 3
    for d, (lower, upper) in enumerate(sides):
        f_up, f_down = flux(c, upper, d), flux(lower, c, d)
        spread = [spread[i] + (f_up[i] - f_down[i]) for i in range(3)]
        laplace = [laplace[i] + (upper[i] + lower[i]) for i in range(3)]
    return [
        c[i] + flow_step * (viscous * (laplace[i] - 6.0 * c[i]) - spread[i]) for i in range(3)
    ]


def both_ways(fields, step, axis):
    n = fields[0].shape[axis]
    return (
        [pltpu.roll(v, step, axis) for v in fields],
        [pltpu.roll(v, n - step, axis) for v in fields],
    )


def runge_kutta(near):
    def sample(e):
        weights = [(jnp.maximum(-v, 0.0), 1.0 - jnp.abs(v), jnp.maximum(v, 0.0)) for v in e]
        total = [0.0] * 3
        for dx in range(3):
            plane = [0.0] * 3
            for dy in range(3):
                for i in range(3):
                    line = sum(weights[2][dz] * near(i, dx, dy, dz) for dz in range(3))
                    plane[i] = plane[i] + weights[1][dy] * line
            total = [total[i] + weights[0][dx] * plane[i] for i in range(3)]
        return total

    k1 = [near(i, 1, 1, 1) for i in range(3)]
    k2 = sample([(0.5 * trace_step) * v for v in k1])
    k3 = sample([(0.5 * trace_step) * v for v in k2])
    k4 = sample([trace_step * v for v in k3])
    return [
        (trace_step / 6.0) * (k1[i] + 2.0 * k2[i] + 2.0 * k3[i] + k4[i]) for i in range(3)
    ]


def points_of(yrecv, slot):
    s, r = divmod(slot, CAP)
    rows = yrecv[s, PT_ROW + 4 * r : PT_ROW + 4 * r + 4, :].astype(jnp.int32)
    return [rows[k : k + 1] for k in range(4)]


def at_edge(z):
    return (z < 2) | (z >= CZ - 2)


def lanes_of(table, index):
    return jnp.take_along_axis(table, index, axis=1, mode="promise_in_bounds")


def main_kernel(own, xlo, xhi, edges, yrecv, fresh, traced, strip, whole, near, table):
    lane = lax.broadcasted_iota(jnp.int32, (LY, CZ), 1)
    strips = [jnp.zeros((LY, CZ), f32) for _ in range(4)]
    for g in range(N_ALL):
        comp, x = group_of(g)
        whole[g, 0:CY, :] = plane_ref(g, own, xlo, xhi)[...]
        whole[g, CY:LY, :] = edges[g]
        plane = whole[g]
        place = WIDTH * x
        early = pltpu.roll(plane, (place + 2) % CZ, 1)
        late = pltpu.roll(plane, (place + 12) % CZ, 1)
        acc = jnp.where((lane >= place + 2) & (lane < place + 6), early, strips[comp])
        strips[comp] = jnp.where((lane >= place + 8) & (lane < place + 12), late, acc)
    for comp in range(4):
        strip[comp] = strips[comp]

    outside = outside_walls()
    for x in range(CX + 2):
        c = [whole[i * LX + x + 1] for i in range(3)]
        sides = [
            ([whole[i * LX + x] for i in range(3)], [whole[i * LX + x + 2] for i in range(3)]),
            both_ways(c, 1, 0),
            both_ways(c, 1, 1),
        ]
        new = advance(c, whole[N_VEL + x], sides)
        for i in range(3):
            if 1 <= x <= CX:
                fresh[i, x - 1] = new[i][:CY]
            a = jnp.where(outside, 0.0, new[i])
            for dz, field in enumerate((pltpu.roll(a, 1, 1), a, pltpu.roll(a, CZ - 1, 1))):
                near[x, i, 0, dz] = pltpu.roll(field, 1, 0)[:CY]
                near[x, i, 1, dz] = field[:CY]
                near[x, i, 2, dz] = pltpu.roll(field, LY - 1, 0)[:CY]

    for x in range(CX):
        moved = runge_kutta(lambda i, dx, dy, dz: near[x + dx, i, dy, dz])
        for i in range(3):
            table[i, x * CY : (x + 1) * CY, :] = moved[i]

    rows = lax.broadcasted_iota(jnp.int32, (CX * CY, CZ), 0)
    for slot in range(SLOTS):
        sx, sy, sz, steps = points_of(yrecv, slot)
        here = (rows == sx * CY + sy) & (steps > 0) & ~at_edge(sz)
        index = jnp.broadcast_to(sz, (8, CZ))
        for i in range(3):
            got = jnp.concatenate(
                [lanes_of(table[i, 8 * k : 8 * k + 8, :], index) for k in range(CX * CY // 8)], 0
            )
            traced[i, slot : slot + 1, :] = jnp.sum(jnp.where(here, got, 0.0), 0, keepdims=True)


def strip_kernel(strip, zlo, zhi, yrecv, fresh_in, traced_in, fresh, traced):
    lane = lax.broadcasted_iota(jnp.int32, (LY, CZ), 1)
    place = lane % WIDTH
    low, high = zlo[...], zhi[...]
    fields = []
    for comp in range(4):
        before = pltpu.roll(low, (CZ - 4 * comp) % CZ, 1)
        after = pltpu.roll(high, (CZ + 10 - 4 * comp) % CZ, 1)
        own = strip[comp]
        own = jnp.where(place < 2, before, own)
        fields.append(jnp.where((place == 12) | (place == 13), after, own))
    c = fields[:3]
    new = advance(c, fields[3], [both_ways(c, WIDTH, 1), both_ways(c, 1, 0), both_ways(c, 1, 1)])

    column = lax.broadcasted_iota(jnp.int32, (CY, CZ), 1)
    for i in range(3):
        part = new[i][:CY]
        for x in range(CX):
            first = WIDTH * (x + 2)
            left = pltpu.roll(part, (CZ - first - 2) % CZ, 1)
            right = pltpu.roll(part, (2 * CZ - 1 - first - 11) % CZ, 1)
            value = jnp.where(column == CZ - 1, right, fresh_in[i, x])
            fresh[i, x] = jnp.where(column == 0, left, value)

    outside = outside_walls()
    near = {}
    for i in range(3):
        a = jnp.where(outside, 0.0, new[i])
        for dz, field in enumerate((pltpu.roll(a, 1, 1), a, pltpu.roll(a, CZ - 1, 1))):
            shifts = (pltpu.roll(field, 1, 0), field, pltpu.roll(field, LY - 1, 0))
            for dy, shifted in enumerate(shifts):
                part = shifted[:CY]
                near[i, 0, dy, dz] = pltpu.roll(part, WIDTH, 1)
                near[i, 1, dy, dz] = part
                near[i, 2, dy, dz] = pltpu.roll(part, CZ - WIDTH, 1)
    moved = runge_kutta(lambda *key: near[key])

    rows = lax.broadcasted_iota(jnp.int32, (CY, CZ), 0)
    for slot in range(SLOTS):
        sx, sy, sz, steps = points_of(yrecv, slot)
        here = (rows == sy) & (steps > 0) & at_edge(sz)
        offset = jnp.where(sz < 2, sz + 2, sz - (CZ - 2) + 10)
        index = jnp.where(at_edge(sz), WIDTH * (sx + 2) + offset, 0)
        index = jnp.broadcast_to(index, (8, CZ))
        for i in range(3):
            got = jnp.concatenate([lanes_of(moved[i][8 * k : 8 * k + 8], index) for k in range(2)], 0)
            value = jnp.sum(jnp.where(here, got, 0.0), 0, keepdims=True)
            traced[i, slot : slot + 1, :] = traced_in[i, slot : slot + 1, :] + value


def shards(velocity, viscosity, counts, destination, seeds, substeps):
    def ring(axis):
        n = lax.axis_size(axis)
        forward = [(i, (i + 1) % n) for i in range(n)]
        return forward, [(b, a) for a, b in forward]

    message = shape(7, CY, CZ)
    own = jnp.concatenate([velocity.reshape(3 * CX, CY, CZ), viscosity], 0)
    to_high, to_low, base = call(
        prepare_kernel, (message, message, shape(TILES, ROWS, CZ)), [SMEM, SMEM] + [VMEM] * 3
    )(
        counts,
        destination.reshape(BLOCKS),
        jnp.swapaxes(seeds.reshape(BLOCKS, 3, CZ), 0, 1),
        substeps.reshape(BLOCKS, CZ),
        own,
    )
    forward, backward = ring("wide")
    xlo = lax.ppermute(to_high, "wide", forward)
    xhi = lax.ppermute(to_low, "wide", backward)
    ymsg = call(y_kernel, shape(TILES, ROWS, CZ), [VMEM] * 3)(base, xlo, xhi)
    yrecv = lax.all_to_all(ymsg, "tile", split_axis=0, concat_axis=0, tiled=True)
    zpart = call(z_kernel, shape(CY, CZ), [VMEM] * 3, flops=1 << 20, moved=1 << 20)(own, xlo, xhi)
    edges, zmsg = call(
        edge_rows_kernel, (shape(N_ALL, 8, CZ), shape(LY, CZ)), [VMEM] * 2
    )(yrecv, zpart)
    forward, backward = ring("sec")
    zlo = lax.ppermute(zmsg, "sec", forward)
    zhi = lax.ppermute(zmsg, "sec", backward)
    fresh, traced, strip = call(
        main_kernel,
        (shape(3, CX, CY, CZ), shape(3, SLOTS, CZ), shape(4, LY, CZ)),
        [VMEM] * 5,
        [
            pltpu.VMEM((N_ALL, LY, CZ), f32),
            pltpu.VMEM((CX + 2, 3, 3, 3, CY, CZ), f32),
            pltpu.VMEM((3, CX * CY, CZ), f32),
        ],
        flops=1 << 22,
        moved=1 << 23,
    )(own, xlo, xhi, edges, yrecv)
    fresh, traced = call(
        strip_kernel, (shape(3, CX, CY, CZ), shape(3, SLOTS, CZ)), [VMEM] * 6
    )(strip, zlo, zhi, yrecv, fresh, traced)
    return fresh, jnp.swapaxes(traced, 0, 1)[None, None, None]


def solution(mesh):
    in_specs = (
        P(None, "wide", "tile", "sec"),
        P("wide", "tile", "sec"),
        P("wide", "sec", "tile"),
        P("wide", "sec", "tile", None),
        P("wide", "sec", "tile", None, None, None),
        P("wide", "sec", "tile", None, None),
    )
    out_specs = (P(None, "wide", "tile", "sec"), P("wide", "sec", "tile", None, None, None))

    return jax.shard_map(shards, mesh=mesh, in_specs=in_specs, out_specs=out_specs, check_vma=False)
```

```python
import jax
import jax.numpy as jnp
from jax import lax
from jax.experimental import pallas as pl
from jax.experimental.pallas import tpu as pltpu
from jax.sharding import PartitionSpec as P


CAP = 2
CX, CY, CZ = 4, 16, 128
TILES = 4
BLOCKS = 4
SLOTS = TILES * CAP
LX = CX + 4
LY = 24
N_VEL = 3 * LX
N_ALL = N_VEL + CX + 2
HALO_ROWS = 26
PT_ROW = 56
ROWS = 64
WIDTH = CZ // LX

flow_step = 0.2
trace_step = 1.25

VMEM = pl.BlockSpec(memory_space=pltpu.VMEM)
SMEM = pl.BlockSpec(memory_space=pltpu.SMEM)
f32 = jnp.float32


def call(kernel, out_shape, in_specs, scratch=(), flops=0, moved=0):
    return pl.pallas_call(
        kernel,
        out_shape=out_shape,
        in_specs=in_specs,
        out_specs=jax.tree.map(lambda _: VMEM, out_shape),
        scratch_shapes=list(scratch),
        compiler_params=pltpu.CompilerParams(vmem_limit_bytes=8 << 20),
        cost_estimate=pl.CostEstimate(flops=flops, bytes_accessed=moved, transcendentals=0),
    )


def shape(*dims):
    return jax.ShapeDtypeStruct(dims, f32)


def group_of(group):
    if group < N_VEL:
        return divmod(group, LX)
    return 3, group - N_VEL + 1


def is_even(axis):
    return lax.axis_index(axis) % 2 == 0


def plane_rows(group, first, size, own, even_first, odd_first):
    comp, x = group_of(group)
    rows = slice(first, first + size)
    if 2 <= x < 2 + CX:
        return own[CX * comp + x - 2, rows, :]
    index = 6 if comp == 3 else 2 * comp + x % 2
    first_is_odd = is_even("wide") if x < 2 else ~is_even("wide")
    return jnp.where(first_is_odd, odd_first[index, rows, :], even_first[index, rows, :])


def inner(group):
    return 2 <= group_of(group)[1] < 2 + CX


def halo_rows(group):
    kind = [g for g in range(N_ALL) if inner(g) == inner(group)]
    first = HALO_ROWS if inner(group) else 0
    vels = [g for g in kind if g < N_VEL]
    if group < N_VEL:
        return first + 2 * kind.index(group), 2
    return first + len(vels) + kind.index(group), 1


def next_tiles():
    tile = lax.axis_index("tile")
    return (tile + 1) % TILES, (tile + TILES - 1) % TILES


def x_kernel(own, odd_first, even_first):
    even = is_even("wide")
    for c in range(4):
        for k in range(2 if c < 3 else 1):
            high = own[CX * c + (CX - 2 + k if c < 3 else CX - 1)]
            low = own[CX * c + k]
            odd_first[2 * c + k] = jnp.where(even, low, high)
            even_first[2 * c + k] = jnp.where(even, high, low)


def points_kernel(dest, counts, seeds, substeps, own, out):
    total = jnp.broadcast_to(counts[0], (4, CZ))
    live = [b < total for b in range(BLOCKS)]
    ranks = []
    for b in range(BLOCKS):
        rank = jnp.int32(0)
        for a in range(b):
            rank = rank + jnp.where(dest[a] == dest[b], 1, 0)
        ranks.append(rank)
    payload = [
        jnp.concatenate([seeds[c, b : b + 1, :] for c in range(3)] + [substeps[b : b + 1, :]], 0)
        for b in range(BLOCKS)
    ]
    for d in range(TILES):
        for r in range(CAP):
            slot = jnp.zeros((4, CZ), jnp.int32)
            for b in range(BLOCKS):
                chosen = live[b] & (dest[b] == d) & (ranks[b] == r)
                slot = jnp.where(chosen, payload[b], slot)
            out[d, PT_ROW + 4 * r : PT_ROW + 4 * r + 4, :] = slot.astype(f32)
    up, down = next_tiles()
    for g in range(N_ALL):
        if inner(g):
            row, n = halo_rows(g)
            out[up, row : row + n, :] = plane_rows(g, CY - n, n, own, None, None)
            out[down, row : row + n, :] = plane_rows(g, 0, n, own, None, None)


def y_kernel(base, even_first, odd_first, out):
    out[...] = base[...]
    up, down = next_tiles()
    for g in range(N_ALL):
        if not inner(g):
            row, n = halo_rows(g)
            out[up, row : row + n, :] = plane_rows(g, CY - n, n, None, even_first, odd_first)
            out[down, row : row + n, :] = plane_rows(g, 0, n, None, even_first, odd_first)


def columns(part, group, lane, acc):
    comp, x = group_of(group)
    place = WIDTH * x + 4 * comp
    moved = pltpu.roll(part, (place + 2) % CZ, 1)
    return jnp.where((lane >= place) & (lane < place + 4), moved, acc)


def z_kernel(own, even_first, odd_first, out):
    lane = lax.broadcasted_iota(jnp.int32, (CY, CZ), 1)
    acc = jnp.zeros((CY, CZ), f32)
    for g in range(N_ALL):
        acc = columns(plane_rows(g, 0, CY, own, even_first, odd_first), g, lane, acc)
    out[...] = acc


def edge_rows_kernel(yrecv, zpart, edges, zmsg):
    tile = lax.axis_index("tile")
    below = jnp.maximum(tile - 1, 0)
    above = jnp.minimum(tile + 1, TILES - 1)
    lane = lax.broadcasted_iota(jnp.int32, (8, CZ), 1)
    acc = jnp.zeros((8, CZ), f32)
    for g in range(N_ALL):
        row, n = halo_rows(g)
        high = jnp.where(tile < TILES - 1, yrecv[above, row : row + n, :], 0.0)
        low = jnp.where(tile > 0, yrecv[below, row : row + n, :], 0.0)
        edge = jnp.concatenate([high, jnp.zeros((8 - 2 * n, CZ), f32), low], 0)
        edges[g] = edge
        acc = columns(edge, g, lane, acc)
    zmsg[0:CY, :] = zpart[...]
    zmsg[CY:LY, :] = acc


def outside_walls():
    tile = lax.axis_index("tile")
    row = lax.broadcasted_iota(jnp.int32, (LY, CZ), 0)
    return ((tile == 0) & (row == LY - 1)) | ((tile == TILES - 1) & (row == CY))


def flux(one, two, d):
    both = one[d] + two[d]
    return [0.25 * (one[i] + two[i]) * both for i in range(3)]


def advance(c, viscous, sides):
    spread = [0.0] * 3
    laplace = [0.0] * 3
    for d, (lower, upper) in enumerate(sides):
        f_up, f_down = flux(c, upper, d), flux(lower, c, d)
        spread = [spread[i] + (f_up[i] - f_down[i]) for i in range(3)]
        laplace = [laplace[i] + (upper[i] + lower[i]) for i in range(3)]
    return [
        c[i] + flow_step * (viscous * (laplace[i] - 6.0 * c[i]) - spread[i]) for i in range(3)
    ]


def both_ways(fields, step, axis):
    n = fields[0].shape[axis]
    return (
        [pltpu.roll(v, step, axis) for v in fields],
        [pltpu.roll(v, n - step, axis) for v in fields],
    )


def runge_kutta(near):
    def sample(e):
        weights = [(jnp.maximum(-v, 0.0), 1.0 - jnp.abs(v), jnp.maximum(v, 0.0)) for v in e]
        total = [0.0] * 3
        for dx in range(3):
            plane = [0.0] * 3
            for dy in range(3):
                for i in range(3):
                    line = sum(weights[2][dz] * near(i, dx, dy, dz) for dz in range(3))
                    plane[i] = plane[i] + weights[1][dy] * line
            total = [total[i] + weights[0][dx] * plane[i] for i in range(3)]
        return total

    k1 = [near(i, 1, 1, 1) for i in range(3)]
    k2 = sample([(0.5 * trace_step) * v for v in k1])
    k3 = sample([(0.5 * trace_step) * v for v in k2])
    k4 = sample([trace_step * v for v in k3])
    return [
        (trace_step / 6.0) * (k1[i] + 2.0 * k2[i] + 2.0 * k3[i] + k4[i]) for i in range(3)
    ]


def points_of(yrecv, slot):
    s, r = divmod(slot, CAP)
    rows = yrecv[s, PT_ROW + 4 * r : PT_ROW + 4 * r + 4, :].astype(jnp.int32)
    return [rows[k : k + 1] for k in range(4)]


def at_edge(z):
    return (z < 2) | (z >= CZ - 2)


def lanes_of(table, index):
    return jnp.take_along_axis(table, index, axis=1, mode="promise_in_bounds")


def main_kernel(own, even_first, odd_first, edges, yrecv, fresh, traced, strip, whole, near, table):
    lane = lax.broadcasted_iota(jnp.int32, (LY, CZ), 1)
    strips = [jnp.zeros((LY, CZ), f32) for _ in range(4)]
    for g in range(N_ALL):
        comp, x = group_of(g)
        whole[g, 0:CY, :] = plane_rows(g, 0, CY, own, even_first, odd_first)
        whole[g, CY:LY, :] = edges[g]
        plane = whole[g]
        place = WIDTH * x
        early = pltpu.roll(plane, (place + 2) % CZ, 1)
        late = pltpu.roll(plane, (place + 12) % CZ, 1)
        acc = jnp.where((lane >= place + 2) & (lane < place + 6), early, strips[comp])
        strips[comp] = jnp.where((lane >= place + 8) & (lane < place + 12), late, acc)
    for comp in range(4):
        strip[comp] = strips[comp]

    outside = outside_walls()
    for x in range(CX + 2):
        c = [whole[i * LX + x + 1] for i in range(3)]
        sides = [
            ([whole[i * LX + x] for i in range(3)], [whole[i * LX + x + 2] for i in range(3)]),
            both_ways(c, 1, 0),
            both_ways(c, 1, 1),
        ]
        new = advance(c, whole[N_VEL + x], sides)
        for i in range(3):
            if 1 <= x <= CX:
                fresh[i, x - 1] = new[i][:CY]
            a = jnp.where(outside, 0.0, new[i])
            for dz, field in enumerate((pltpu.roll(a, 1, 1), a, pltpu.roll(a, CZ - 1, 1))):
                near[x, i, 0, dz] = pltpu.roll(field, 1, 0)[:CY]
                near[x, i, 1, dz] = field[:CY]
                near[x, i, 2, dz] = pltpu.roll(field, LY - 1, 0)[:CY]

    for x in range(CX):
        moved = runge_kutta(lambda i, dx, dy, dz: near[x + dx, i, dy, dz])
        for i in range(3):
            table[i, x * CY : (x + 1) * CY, :] = moved[i]

    rows = lax.broadcasted_iota(jnp.int32, (CX * CY, CZ), 0)
    for slot in range(SLOTS):
        sx, sy, sz, steps = points_of(yrecv, slot)
        here = (rows == sx * CY + sy) & (steps > 0) & ~at_edge(sz)
        index = jnp.broadcast_to(sz, (8, CZ))
        for i in range(3):
            got = jnp.concatenate(
                [lanes_of(table[i, 8 * k : 8 * k + 8, :], index) for k in range(CX * CY // 8)], 0
            )
            traced[i, slot : slot + 1, :] = jnp.sum(jnp.where(here, got, 0.0), 0, keepdims=True)


def strip_kernel(strip, even_first, odd_first, yrecv, fresh_in, traced_in, fresh, traced):
    lane = lax.broadcasted_iota(jnp.int32, (LY, CZ), 1)
    place = lane % WIDTH
    even = is_even("sec")
    low = jnp.where(even, odd_first[...], even_first[...])
    high = jnp.where(even, even_first[...], odd_first[...])
    fields = []
    for comp in range(4):
        before = pltpu.roll(low, (CZ - 4 * comp) % CZ, 1)
        after = pltpu.roll(high, (CZ + 10 - 4 * comp) % CZ, 1)
        own = strip[comp]
        own = jnp.where(place < 2, before, own)
        fields.append(jnp.where((place == 12) | (place == 13), after, own))
    c = fields[:3]
    new = advance(c, fields[3], [both_ways(c, WIDTH, 1), both_ways(c, 1, 0), both_ways(c, 1, 1)])

    column = lax.broadcasted_iota(jnp.int32, (CY, CZ), 1)
    for i in range(3):
        part = new[i][:CY]
        for x in range(CX):
            first = WIDTH * (x + 2)
            left = pltpu.roll(part, (CZ - first - 2) % CZ, 1)
            right = pltpu.roll(part, (2 * CZ - 1 - first - 11) % CZ, 1)
            value = jnp.where(column == CZ - 1, right, fresh_in[i, x])
            fresh[i, x] = jnp.where(column == 0, left, value)

    outside = outside_walls()
    near = {}
    for i in range(3):
        a = jnp.where(outside, 0.0, new[i])
        for dz, field in enumerate((pltpu.roll(a, 1, 1), a, pltpu.roll(a, CZ - 1, 1))):
            shifts = (pltpu.roll(field, 1, 0), field, pltpu.roll(field, LY - 1, 0))
            for dy, shifted in enumerate(shifts):
                part = shifted[:CY]
                near[i, 0, dy, dz] = pltpu.roll(part, WIDTH, 1)
                near[i, 1, dy, dz] = part
                near[i, 2, dy, dz] = pltpu.roll(part, CZ - WIDTH, 1)
    moved = runge_kutta(lambda *key: near[key])

    rows = lax.broadcasted_iota(jnp.int32, (CY, CZ), 0)
    for slot in range(SLOTS):
        sx, sy, sz, steps = points_of(yrecv, slot)
        here = (rows == sy) & (steps > 0) & at_edge(sz)
        offset = jnp.where(sz < 2, sz + 2, sz - (CZ - 2) + 10)
        index = jnp.where(at_edge(sz), WIDTH * (sx + 2) + offset, 0)
        index = jnp.broadcast_to(index, (8, CZ))
        for i in range(3):
            got = jnp.concatenate([lanes_of(moved[i][8 * k : 8 * k + 8], index) for k in range(2)], 0)
            value = jnp.sum(jnp.where(here, got, 0.0), 0, keepdims=True)
            traced[i, slot : slot + 1, :] = traced_in[i, slot : slot + 1, :] + value


def shards(velocity, viscosity, counts, destination, seeds, substeps):
    def swap(value, axis, first):
        n = lax.axis_size(axis)
        pairs = [(i, (i + 1) % n) for i in range(first, n, 2)]
        return lax.ppermute(value, axis, pairs + [(b, a) for a, b in pairs])

    message = shape(7, CY, CZ)
    own = jnp.concatenate([velocity.reshape(3 * CX, CY, CZ), viscosity], 0)
    x_odd, x_even = call(x_kernel, (message, message), [VMEM])(own)
    x_odd = swap(x_odd, "wide", 1)
    x_even = swap(x_even, "wide", 0)
    base = call(
        points_kernel, shape(TILES, ROWS, CZ), [SMEM] + [VMEM] * 4, flops=1 << 20, moved=1 << 20
    )(
        destination.reshape(BLOCKS),
        counts,
        jnp.swapaxes(seeds.reshape(BLOCKS, 3, CZ), 0, 1),
        substeps.reshape(BLOCKS, CZ),
        own,
    )
    ymsg = call(y_kernel, shape(TILES, ROWS, CZ), [VMEM] * 3)(base, x_even, x_odd)
    yrecv = lax.all_to_all(ymsg, "tile", split_axis=0, concat_axis=0, tiled=True)
    zpart = call(z_kernel, shape(CY, CZ), [VMEM] * 3, flops=1 << 20, moved=1 << 20)(
        own, x_even, x_odd
    )
    edges, zmsg = call(
        edge_rows_kernel, (shape(N_ALL, 8, CZ), shape(LY, CZ)), [VMEM] * 2
    )(yrecv, zpart)
    z_odd = swap(zmsg, "sec", 1)
    z_even = swap(zmsg, "sec", 0)
    fresh, traced, strip = call(
        main_kernel,
        (shape(3, CX, CY, CZ), shape(3, SLOTS, CZ), shape(4, LY, CZ)),
        [VMEM] * 5,
        [
            pltpu.VMEM((N_ALL, LY, CZ), f32),
            pltpu.VMEM((CX + 2, 3, 3, 3, CY, CZ), f32),
            pltpu.VMEM((3, CX * CY, CZ), f32),
        ],
        flops=1 << 22,
        moved=1 << 23,
    )(own, x_even, x_odd, edges, yrecv)
    fresh, traced = call(
        strip_kernel, (shape(3, CX, CY, CZ), shape(3, SLOTS, CZ)), [VMEM] * 6
    )(strip, z_even, z_odd, yrecv, fresh, traced)
    return fresh, jnp.swapaxes(traced, 0, 1)[None, None, None]


def solution(mesh):
    in_specs = (
        P(None, "wide", "tile", "sec"),
        P("wide", "tile", "sec"),
        P("wide", "sec", "tile"),
        P("wide", "sec", "tile", None),
        P("wide", "sec", "tile", None, None, None),
        P("wide", "sec", "tile", None, None),
    )
    out_specs = (P(None, "wide", "tile", "sec"), P("wide", "sec", "tile", None, None, None))

    return jax.shard_map(shards, mesh=mesh, in_specs=in_specs, out_specs=out_specs, check_vma=False)
```

```python
import jax
import jax.numpy as jnp
from jax import lax
from jax.experimental import pallas as pl
from jax.experimental.pallas import tpu as pltpu
from jax.sharding import PartitionSpec as P


CAP = 2
CX, CY, CZ = 4, 16, 128
TILES = 4
BLOCKS = 4
SLOTS = TILES * CAP
LX = CX + 4
LY = 24
N_VEL = 3 * LX
N_ALL = N_VEL + CX + 2
HALO_ROWS = 26
PT_ROW = 56
ROWS = 64
WIDTH = CZ // LX
RUN = 8

flow_step = 0.2
trace_step = 1.25

VMEM = pl.BlockSpec(memory_space=pltpu.VMEM)
SMEM = pl.BlockSpec(memory_space=pltpu.SMEM)
f32 = jnp.float32


def call(kernel, out_shape, in_specs, scratch=(), flops=0, moved=0):
    return pl.pallas_call(
        kernel,
        out_shape=out_shape,
        in_specs=in_specs,
        out_specs=jax.tree.map(lambda _: VMEM, out_shape),
        scratch_shapes=list(scratch),
        compiler_params=pltpu.CompilerParams(vmem_limit_bytes=8 << 20),
        cost_estimate=pl.CostEstimate(flops=flops, bytes_accessed=moved, transcendentals=0),
    )


def shape(*dims):
    return jax.ShapeDtypeStruct(dims, f32)


def group_of(group):
    if group < N_VEL:
        return divmod(group, LX)
    return 3, group - N_VEL + 1


def is_even(axis):
    return lax.axis_index(axis) % 2 == 0


def of_even_pair(axis, early, late):
    return jnp.where(lax.axis_index(axis) % RUN < RUN // 2, early, late)


def plane_rows(group, first, size, own, early, late, odd):
    comp, x = group_of(group)
    rows = slice(first, first + size)
    if 2 <= x < 2 + CX:
        return own[CX * comp + x - 2, rows, :]
    index = 6 if comp == 3 else 2 * comp + x % 2
    from_odd = is_even("wide") if x < 2 else ~is_even("wide")
    even = of_even_pair("wide", early[index, rows, :], late[index, rows, :])
    return jnp.where(from_odd, odd[index, rows, :], even)


def inner(group):
    return 2 <= group_of(group)[1] < 2 + CX


def halo_rows(group):
    kind = [g for g in range(N_ALL) if inner(g) == inner(group)]
    first = HALO_ROWS if inner(group) else 0
    vels = [g for g in kind if g < N_VEL]
    if group < N_VEL:
        return first + 2 * kind.index(group), 2
    return first + len(vels) + kind.index(group), 1


def next_tiles():
    tile = lax.axis_index("tile")
    return (tile + 1) % TILES, (tile + TILES - 1) % TILES


def x_kernel(own, odd_first, even_first):
    even = is_even("wide")
    for c in range(4):
        for k in range(2 if c < 3 else 1):
            high = own[CX * c + (CX - 2 + k if c < 3 else CX - 1)]
            low = own[CX * c + k]
            odd_first[2 * c + k] = jnp.where(even, low, high)
            even_first[2 * c + k] = jnp.where(even, high, low)


def points_kernel(dest, counts, seeds, substeps, own, out):
    total = jnp.broadcast_to(counts[0], (4, CZ))
    live = [b < total for b in range(BLOCKS)]
    ranks = []
    for b in range(BLOCKS):
        rank = jnp.int32(0)
        for a in range(b):
            rank = rank + jnp.where(dest[a] == dest[b], 1, 0)
        ranks.append(rank)
    payload = [
        jnp.concatenate([seeds[c, b : b + 1, :] for c in range(3)] + [substeps[b : b + 1, :]], 0)
        for b in range(BLOCKS)
    ]
    for d in range(TILES):
        for r in range(CAP):
            slot = jnp.zeros((4, CZ), jnp.int32)
            for b in range(BLOCKS):
                chosen = live[b] & (dest[b] == d) & (ranks[b] == r)
                slot = jnp.where(chosen, payload[b], slot)
            out[d, PT_ROW + 4 * r : PT_ROW + 4 * r + 4, :] = slot.astype(f32)
    up, down = next_tiles()
    for g in range(N_ALL):
        if inner(g):
            row, n = halo_rows(g)
            out[up, row : row + n, :] = plane_rows(g, CY - n, n, own, None, None, None)
            out[down, row : row + n, :] = plane_rows(g, 0, n, own, None, None, None)


def y_kernel(base, early, late, odd, out):
    out[...] = base[...]
    up, down = next_tiles()
    for g in range(N_ALL):
        if not inner(g):
            row, n = halo_rows(g)
            out[up, row : row + n, :] = plane_rows(g, CY - n, n, None, early, late, odd)
            out[down, row : row + n, :] = plane_rows(g, 0, n, None, early, late, odd)


def columns(part, group, lane, acc):
    comp, x = group_of(group)
    place = WIDTH * x + 4 * comp
    moved = pltpu.roll(part, (place + 2) % CZ, 1)
    return jnp.where((lane >= place) & (lane < place + 4), moved, acc)


def z_kernel(own, early, late, odd, out):
    lane = lax.broadcasted_iota(jnp.int32, (CY, CZ), 1)
    acc = jnp.zeros((CY, CZ), f32)
    for g in range(N_ALL):
        acc = columns(plane_rows(g, 0, CY, own, early, late, odd), g, lane, acc)
    out[...] = acc


def edge_rows_kernel(yrecv, zpart, edges, zmsg):
    tile = lax.axis_index("tile")
    below = jnp.maximum(tile - 1, 0)
    above = jnp.minimum(tile + 1, TILES - 1)
    lane = lax.broadcasted_iota(jnp.int32, (8, CZ), 1)
    acc = jnp.zeros((8, CZ), f32)
    for g in range(N_ALL):
        row, n = halo_rows(g)
        high = jnp.where(tile < TILES - 1, yrecv[above, row : row + n, :], 0.0)
        low = jnp.where(tile > 0, yrecv[below, row : row + n, :], 0.0)
        edge = jnp.concatenate([high, jnp.zeros((8 - 2 * n, CZ), f32), low], 0)
        edges[g] = edge
        acc = columns(edge, g, lane, acc)
    zmsg[0:CY, :] = zpart[...]
    zmsg[CY:LY, :] = acc


def outside_walls():
    tile = lax.axis_index("tile")
    row = lax.broadcasted_iota(jnp.int32, (LY, CZ), 0)
    return ((tile == 0) & (row == LY - 1)) | ((tile == TILES - 1) & (row == CY))


def flux(one, two, d):
    both = one[d] + two[d]
    return [0.25 * (one[i] + two[i]) * both for i in range(3)]


def advance(c, viscous, sides):
    spread = [0.0] * 3
    laplace = [0.0] * 3
    for d, (lower, upper) in enumerate(sides):
        f_up, f_down = flux(c, upper, d), flux(lower, c, d)
        spread = [spread[i] + (f_up[i] - f_down[i]) for i in range(3)]
        laplace = [laplace[i] + (upper[i] + lower[i]) for i in range(3)]
    return [
        c[i] + flow_step * (viscous * (laplace[i] - 6.0 * c[i]) - spread[i]) for i in range(3)
    ]


def both_ways(fields, step, axis):
    n = fields[0].shape[axis]
    return (
        [pltpu.roll(v, step, axis) for v in fields],
        [pltpu.roll(v, n - step, axis) for v in fields],
    )


def runge_kutta(near):
    def sample(e):
        weights = [(jnp.maximum(-v, 0.0), 1.0 - jnp.abs(v), jnp.maximum(v, 0.0)) for v in e]
        total = [0.0] * 3
        for dx in range(3):
            plane = [0.0] * 3
            for dy in range(3):
                for i in range(3):
                    line = sum(weights[2][dz] * near(i, dx, dy, dz) for dz in range(3))
                    plane[i] = plane[i] + weights[1][dy] * line
            total = [total[i] + weights[0][dx] * plane[i] for i in range(3)]
        return total

    k1 = [near(i, 1, 1, 1) for i in range(3)]
    k2 = sample([(0.5 * trace_step) * v for v in k1])
    k3 = sample([(0.5 * trace_step) * v for v in k2])
    k4 = sample([trace_step * v for v in k3])
    return [
        (trace_step / 6.0) * (k1[i] + 2.0 * k2[i] + 2.0 * k3[i] + k4[i]) for i in range(3)
    ]


def points_of(yrecv, slot):
    s, r = divmod(slot, CAP)
    rows = yrecv[s, PT_ROW + 4 * r : PT_ROW + 4 * r + 4, :].astype(jnp.int32)
    return [rows[k : k + 1] for k in range(4)]


def at_edge(z):
    return (z < 2) | (z >= CZ - 2)


def lanes_of(table, index):
    return jnp.take_along_axis(table, index, axis=1, mode="promise_in_bounds")


def main_kernel(own, early, late, odd, edges, yrecv, fresh, traced, strip, whole, near, table):
    lane = lax.broadcasted_iota(jnp.int32, (LY, CZ), 1)
    strips = [jnp.zeros((LY, CZ), f32) for _ in range(4)]
    for g in range(N_ALL):
        comp, x = group_of(g)
        whole[g, 0:CY, :] = plane_rows(g, 0, CY, own, early, late, odd)
        whole[g, CY:LY, :] = edges[g]
        plane = whole[g]
        place = WIDTH * x
        start_columns = pltpu.roll(plane, (place + 2) % CZ, 1)
        end_columns = pltpu.roll(plane, (place + 12) % CZ, 1)
        acc = jnp.where((lane >= place + 2) & (lane < place + 6), start_columns, strips[comp])
        strips[comp] = jnp.where((lane >= place + 8) & (lane < place + 12), end_columns, acc)
    for comp in range(4):
        strip[comp] = strips[comp]

    outside = outside_walls()
    for x in range(CX + 2):
        c = [whole[i * LX + x + 1] for i in range(3)]
        sides = [
            ([whole[i * LX + x] for i in range(3)], [whole[i * LX + x + 2] for i in range(3)]),
            both_ways(c, 1, 0),
            both_ways(c, 1, 1),
        ]
        new = advance(c, whole[N_VEL + x], sides)
        for i in range(3):
            if 1 <= x <= CX:
                fresh[i, x - 1] = new[i][:CY]
            a = jnp.where(outside, 0.0, new[i])
            for dz, field in enumerate((pltpu.roll(a, 1, 1), a, pltpu.roll(a, CZ - 1, 1))):
                near[x, i, 0, dz] = pltpu.roll(field, 1, 0)[:CY]
                near[x, i, 1, dz] = field[:CY]
                near[x, i, 2, dz] = pltpu.roll(field, LY - 1, 0)[:CY]

    for x in range(CX):
        moved = runge_kutta(lambda i, dx, dy, dz: near[x + dx, i, dy, dz])
        for i in range(3):
            table[i, x * CY : (x + 1) * CY, :] = moved[i]

    rows = lax.broadcasted_iota(jnp.int32, (CX * CY, CZ), 0)
    for slot in range(SLOTS):
        sx, sy, sz, steps = points_of(yrecv, slot)
        here = (rows == sx * CY + sy) & (steps > 0) & ~at_edge(sz)
        index = jnp.broadcast_to(sz, (8, CZ))
        for i in range(3):
            got = jnp.concatenate(
                [lanes_of(table[i, 8 * k : 8 * k + 8, :], index) for k in range(CX * CY // 8)], 0
            )
            traced[i, slot : slot + 1, :] = jnp.sum(jnp.where(here, got, 0.0), 0, keepdims=True)


def strip_kernel(strip, early, late, odd, yrecv, fresh_in, traced_in, fresh, traced):
    lane = lax.broadcasted_iota(jnp.int32, (LY, CZ), 1)
    place = lane % WIDTH
    even = is_even("sec")
    from_odd, from_even = odd[...], of_even_pair("sec", early[...], late[...])
    low = jnp.where(even, from_odd, from_even)
    high = jnp.where(even, from_even, from_odd)
    fields = []
    for comp in range(4):
        before = pltpu.roll(low, (CZ - 4 * comp) % CZ, 1)
        after = pltpu.roll(high, (CZ + 10 - 4 * comp) % CZ, 1)
        own = strip[comp]
        own = jnp.where(place < 2, before, own)
        fields.append(jnp.where((place == 12) | (place == 13), after, own))
    c = fields[:3]
    new = advance(c, fields[3], [both_ways(c, WIDTH, 1), both_ways(c, 1, 0), both_ways(c, 1, 1)])

    column = lax.broadcasted_iota(jnp.int32, (CY, CZ), 1)
    for i in range(3):
        part = new[i][:CY]
        for x in range(CX):
            first = WIDTH * (x + 2)
            left = pltpu.roll(part, (CZ - first - 2) % CZ, 1)
            right = pltpu.roll(part, (2 * CZ - 1 - first - 11) % CZ, 1)
            value = jnp.where(column == CZ - 1, right, fresh_in[i, x])
            fresh[i, x] = jnp.where(column == 0, left, value)

    outside = outside_walls()
    near = {}
    for i in range(3):
        a = jnp.where(outside, 0.0, new[i])
        for dz, field in enumerate((pltpu.roll(a, 1, 1), a, pltpu.roll(a, CZ - 1, 1))):
            shifts = (pltpu.roll(field, 1, 0), field, pltpu.roll(field, LY - 1, 0))
            for dy, shifted in enumerate(shifts):
                part = shifted[:CY]
                near[i, 0, dy, dz] = pltpu.roll(part, WIDTH, 1)
                near[i, 1, dy, dz] = part
                near[i, 2, dy, dz] = pltpu.roll(part, CZ - WIDTH, 1)
    moved = runge_kutta(lambda *key: near[key])

    rows = lax.broadcasted_iota(jnp.int32, (CY, CZ), 0)
    for slot in range(SLOTS):
        sx, sy, sz, steps = points_of(yrecv, slot)
        here = (rows == sy) & (steps > 0) & at_edge(sz)
        offset = jnp.where(sz < 2, sz + 2, sz - (CZ - 2) + 10)
        index = jnp.where(at_edge(sz), WIDTH * (sx + 2) + offset, 0)
        index = jnp.broadcast_to(index, (8, CZ))
        for i in range(3):
            got = jnp.concatenate([lanes_of(moved[i][8 * k : 8 * k + 8], index) for k in range(2)], 0)
            value = jnp.sum(jnp.where(here, got, 0.0), 0, keepdims=True)
            traced[i, slot : slot + 1, :] = traced_in[i, slot : slot + 1, :] + value


def shards(velocity, viscosity, counts, destination, seeds, substeps):
    def swap(value, axis, kept):
        n = lax.axis_size(axis)
        pairs = [(i, (i + 1) % n) for i in range(n) if kept(i)]
        return lax.ppermute(value, axis, pairs + [(b, a) for a, b in pairs])

    def exchange(even, odd, axis):
        early = swap(even, axis, lambda i: i % 2 == 0 and i % RUN < RUN // 2)
        odd = swap(odd, axis, lambda i: i % 2 == 1)
        late = swap(even, axis, lambda i: i % 2 == 0 and i % RUN >= RUN // 2)
        return early, late, odd

    message = shape(7, CY, CZ)
    own = jnp.concatenate([velocity.reshape(3 * CX, CY, CZ), viscosity], 0)
    x_odd, x_even = call(x_kernel, (message, message), [VMEM])(own)
    from_x = exchange(x_even, x_odd, "wide")
    base = call(
        points_kernel, shape(TILES, ROWS, CZ), [SMEM] + [VMEM] * 4, flops=1 << 20, moved=1 << 20
    )(
        destination.reshape(BLOCKS),
        counts,
        jnp.swapaxes(seeds.reshape(BLOCKS, 3, CZ), 0, 1),
        substeps.reshape(BLOCKS, CZ),
        own,
    )
    ymsg = call(y_kernel, shape(TILES, ROWS, CZ), [VMEM] * 4)(base, *from_x)
    yrecv = lax.all_to_all(ymsg, "tile", split_axis=0, concat_axis=0, tiled=True)
    zpart = call(z_kernel, shape(CY, CZ), [VMEM] * 4, flops=1 << 20, moved=1 << 20)(own, *from_x)
    edges, zmsg = call(
        edge_rows_kernel, (shape(N_ALL, 8, CZ), shape(LY, CZ)), [VMEM] * 2
    )(yrecv, zpart)
    from_z = exchange(zmsg, zmsg, "sec")
    fresh, traced, strip = call(
        main_kernel,
        (shape(3, CX, CY, CZ), shape(3, SLOTS, CZ), shape(4, LY, CZ)),
        [VMEM] * 6,
        [
            pltpu.VMEM((N_ALL, LY, CZ), f32),
            pltpu.VMEM((CX + 2, 3, 3, 3, CY, CZ), f32),
            pltpu.VMEM((3, CX * CY, CZ), f32),
        ],
        flops=1 << 22,
        moved=1 << 23,
    )(own, *from_x, edges, yrecv)
    fresh, traced = call(
        strip_kernel, (shape(3, CX, CY, CZ), shape(3, SLOTS, CZ)), [VMEM] * 7
    )(strip, *from_z, yrecv, fresh, traced)
    return fresh, jnp.swapaxes(traced, 0, 1)[None, None, None]


def solution(mesh):
    in_specs = (
        P(None, "wide", "tile", "sec"),
        P("wide", "tile", "sec"),
        P("wide", "sec", "tile"),
        P("wide", "sec", "tile", None),
        P("wide", "sec", "tile", None, None, None),
        P("wide", "sec", "tile", None, None),
    )
    out_specs = (P(None, "wide", "tile", "sec"), P("wide", "sec", "tile", None, None, None))

    return jax.shard_map(shards, mesh=mesh, in_specs=in_specs, out_specs=out_specs, check_vma=False)
```

```python
import jax
import jax.numpy as jnp
from jax import lax
from jax.experimental import pallas as pl
from jax.experimental.pallas import tpu as pltpu
from jax.sharding import PartitionSpec as P


CAP = 2
CX, CY, CZ = 4, 16, 128
TILES = 4
BLOCKS = 4
SLOTS = TILES * CAP
LX = CX + 4
LY = 24
N_VEL = 3 * LX
N_ALL = N_VEL + CX + 2
HALO_ROWS = 26
PT_ROW = 56
ROWS = 64
WIDTH = CZ // LX
RUN = 8

flow_step = 0.2
trace_step = 1.25

VMEM = pl.BlockSpec(memory_space=pltpu.VMEM)
SMEM = pl.BlockSpec(memory_space=pltpu.SMEM)
f32 = jnp.float32


def call(kernel, out_shape, in_specs, scratch=(), flops=0, moved=0):
    return pl.pallas_call(
        kernel,
        out_shape=out_shape,
        in_specs=in_specs,
        out_specs=jax.tree.map(lambda _: VMEM, out_shape),
        scratch_shapes=list(scratch),
        compiler_params=pltpu.CompilerParams(vmem_limit_bytes=8 << 20),
        cost_estimate=pl.CostEstimate(flops=flops, bytes_accessed=moved, transcendentals=0),
    )


def shape(*dims):
    return jax.ShapeDtypeStruct(dims, f32)


def group_of(group):
    if group < N_VEL:
        return divmod(group, LX)
    return 3, group - N_VEL + 1


def is_even(axis):
    return lax.axis_index(axis) % 2 == 0


def of_even_pair(axis, early, late):
    return jnp.where(lax.axis_index(axis) % RUN < RUN // 2, early, late)


def plane_rows(group, first, size, own, early, late, odd):
    comp, x = group_of(group)
    rows = slice(first, first + size)
    if 2 <= x < 2 + CX:
        return own[CX * comp + x - 2, rows, :]
    index = 6 if comp == 3 else 2 * comp + x % 2
    from_odd = is_even("wide") if x < 2 else ~is_even("wide")
    even = of_even_pair("wide", early[index, rows, :], late[index, rows, :])
    return jnp.where(from_odd, odd[index, rows, :], even)


def inner(group):
    return 2 <= group_of(group)[1] < 2 + CX


def halo_rows(group):
    kind = [g for g in range(N_ALL) if inner(g) == inner(group)]
    first = HALO_ROWS if inner(group) else 0
    vels = [g for g in kind if g < N_VEL]
    if group < N_VEL:
        return first + 2 * kind.index(group), 2
    return first + len(vels) + kind.index(group), 1


def next_tiles():
    tile = lax.axis_index("tile")
    return (tile + 1) % TILES, (tile + TILES - 1) % TILES


def x_kernel(own, odd_first, even_first):
    even = is_even("wide")
    for c in range(4):
        for k in range(2 if c < 3 else 1):
            high = own[CX * c + (CX - 2 + k if c < 3 else CX - 1)]
            low = own[CX * c + k]
            odd_first[2 * c + k] = jnp.where(even, low, high)
            even_first[2 * c + k] = jnp.where(even, high, low)


def points_kernel(dest, counts, seeds, substeps, own, out):
    total = jnp.broadcast_to(counts[0], (4, CZ))
    live = [b < total for b in range(BLOCKS)]
    ranks = []
    for b in range(BLOCKS):
        rank = jnp.int32(0)
        for a in range(b):
            rank = rank + jnp.where(dest[a] == dest[b], 1, 0)
        ranks.append(rank)
    payload = [
        jnp.concatenate([seeds[c, b : b + 1, :] for c in range(3)] + [substeps[b : b + 1, :]], 0)
        for b in range(BLOCKS)
    ]
    for d in range(TILES):
        for r in range(CAP):
            slot = jnp.zeros((4, CZ), jnp.int32)
            for b in range(BLOCKS):
                chosen = live[b] & (dest[b] == d) & (ranks[b] == r)
                slot = jnp.where(chosen, payload[b], slot)
            out[d, PT_ROW + 4 * r : PT_ROW + 4 * r + 4, :] = slot.astype(f32)
    up, down = next_tiles()
    for g in range(N_ALL):
        if inner(g):
            row, n = halo_rows(g)
            out[up, row : row + n, :] = plane_rows(g, CY - n, n, own, None, None, None)
            out[down, row : row + n, :] = plane_rows(g, 0, n, own, None, None, None)


def y_kernel(base, early, late, odd, out):
    out[...] = base[...]
    up, down = next_tiles()
    for g in range(N_ALL):
        if not inner(g):
            row, n = halo_rows(g)
            out[up, row : row + n, :] = plane_rows(g, CY - n, n, None, early, late, odd)
            out[down, row : row + n, :] = plane_rows(g, 0, n, None, early, late, odd)


def columns(part, group, lane, acc):
    comp, x = group_of(group)
    place = WIDTH * x + 4 * comp
    moved = pltpu.roll(part, (place + 2) % CZ, 1)
    return jnp.where((lane >= place) & (lane < place + 4), moved, acc)


def z_kernel(own, early, late, odd, out):
    lane = lax.broadcasted_iota(jnp.int32, (CY, CZ), 1)
    acc = jnp.zeros((CY, CZ), f32)
    for g in range(N_ALL):
        acc = columns(plane_rows(g, 0, CY, own, early, late, odd), g, lane, acc)
    out[...] = acc


def edge_rows_kernel(yrecv, zpart, edges, zmsg):
    tile = lax.axis_index("tile")
    below = jnp.maximum(tile - 1, 0)
    above = jnp.minimum(tile + 1, TILES - 1)
    lane = lax.broadcasted_iota(jnp.int32, (8, CZ), 1)
    acc = jnp.zeros((8, CZ), f32)
    for g in range(N_ALL):
        row, n = halo_rows(g)
        high = jnp.where(tile < TILES - 1, yrecv[above, row : row + n, :], 0.0)
        low = jnp.where(tile > 0, yrecv[below, row : row + n, :], 0.0)
        edge = jnp.concatenate([high, jnp.zeros((8 - 2 * n, CZ), f32), low], 0)
        edges[g] = edge
        acc = columns(edge, g, lane, acc)
    zmsg[0:CY, :] = zpart[...]
    zmsg[CY:LY, :] = acc


def outside_walls():
    tile = lax.axis_index("tile")
    row = lax.broadcasted_iota(jnp.int32, (LY, CZ), 0)
    return ((tile == 0) & (row == LY - 1)) | ((tile == TILES - 1) & (row == CY))


def flux(one, two, d):
    both = one[d] + two[d]
    return [0.25 * (one[i] + two[i]) * both for i in range(3)]


def advance(c, viscous, sides):
    spread = [0.0] * 3
    laplace = [0.0] * 3
    for d, (lower, upper) in enumerate(sides):
        f_up, f_down = flux(c, upper, d), flux(lower, c, d)
        spread = [spread[i] + (f_up[i] - f_down[i]) for i in range(3)]
        laplace = [laplace[i] + (upper[i] + lower[i]) for i in range(3)]
    return [
        c[i] + flow_step * (viscous * (laplace[i] - 6.0 * c[i]) - spread[i]) for i in range(3)
    ]


def both_ways(fields, step, axis):
    n = fields[0].shape[axis]
    return (
        [pltpu.roll(v, step, axis) for v in fields],
        [pltpu.roll(v, n - step, axis) for v in fields],
    )


def runge_kutta(near):
    def sample(e):
        weights = [(jnp.maximum(-v, 0.0), 1.0 - jnp.abs(v), jnp.maximum(v, 0.0)) for v in e]
        total = [0.0] * 3
        for dx in range(3):
            plane = [0.0] * 3
            for dy in range(3):
                for i in range(3):
                    line = sum(weights[2][dz] * near(i, dx, dy, dz) for dz in range(3))
                    plane[i] = plane[i] + weights[1][dy] * line
            total = [total[i] + weights[0][dx] * plane[i] for i in range(3)]
        return total

    k1 = [near(i, 1, 1, 1) for i in range(3)]
    k2 = sample([(0.5 * trace_step) * v for v in k1])
    k3 = sample([(0.5 * trace_step) * v for v in k2])
    k4 = sample([trace_step * v for v in k3])
    return [
        (trace_step / 6.0) * (k1[i] + 2.0 * k2[i] + 2.0 * k3[i] + k4[i]) for i in range(3)
    ]


def points_of(yrecv, slot):
    s, r = divmod(slot, CAP)
    rows = yrecv[s, PT_ROW + 4 * r : PT_ROW + 4 * r + 4, :].astype(jnp.int32)
    return [rows[k : k + 1] for k in range(4)]


def at_edge(z):
    return (z < 2) | (z >= CZ - 2)


def lanes_of(table, index):
    return jnp.take_along_axis(table, index, axis=1, mode="promise_in_bounds")


def main_kernel(own, early, late, odd, edges, yrecv, fresh, traced, strip, whole, near, table):
    lane = lax.broadcasted_iota(jnp.int32, (LY, CZ), 1)
    strips = [jnp.zeros((LY, CZ), f32) for _ in range(4)]
    for g in range(N_ALL):
        comp, x = group_of(g)
        whole[g, 0:CY, :] = plane_rows(g, 0, CY, own, early, late, odd)
        whole[g, CY:LY, :] = edges[g]
        plane = whole[g]
        place = WIDTH * x
        start_columns = pltpu.roll(plane, (place + 2) % CZ, 1)
        end_columns = pltpu.roll(plane, (place + 12) % CZ, 1)
        acc = jnp.where((lane >= place + 2) & (lane < place + 6), start_columns, strips[comp])
        strips[comp] = jnp.where((lane >= place + 8) & (lane < place + 12), end_columns, acc)
    for comp in range(4):
        strip[comp] = strips[comp]

    outside = outside_walls()
    for x in range(CX + 2):
        c = [whole[i * LX + x + 1] for i in range(3)]
        sides = [
            ([whole[i * LX + x] for i in range(3)], [whole[i * LX + x + 2] for i in range(3)]),
            both_ways(c, 1, 0),
            both_ways(c, 1, 1),
        ]
        new = advance(c, whole[N_VEL + x], sides)
        for i in range(3):
            if 1 <= x <= CX:
                fresh[i, x - 1] = new[i][:CY]
            a = jnp.where(outside, 0.0, new[i])
            for dz, field in enumerate((pltpu.roll(a, 1, 1), a, pltpu.roll(a, CZ - 1, 1))):
                near[x, i, 0, dz] = pltpu.roll(field, 1, 0)[:CY]
                near[x, i, 1, dz] = field[:CY]
                near[x, i, 2, dz] = pltpu.roll(field, LY - 1, 0)[:CY]

    for x in range(CX):
        moved = runge_kutta(lambda i, dx, dy, dz: near[x + dx, i, dy, dz])
        for i in range(3):
            table[i, x * CY : (x + 1) * CY, :] = moved[i]

    rows = lax.broadcasted_iota(jnp.int32, (CX * CY, CZ), 0)
    for slot in range(SLOTS):
        sx, sy, sz, steps = points_of(yrecv, slot)
        here = (rows == sx * CY + sy) & (steps > 0) & ~at_edge(sz)
        index = jnp.broadcast_to(sz, (8, CZ))
        for i in range(3):
            got = jnp.concatenate(
                [lanes_of(table[i, 8 * k : 8 * k + 8, :], index) for k in range(CX * CY // 8)], 0
            )
            traced[i, slot : slot + 1, :] = jnp.sum(jnp.where(here, got, 0.0), 0, keepdims=True)


def strip_kernel(strip, from_even_pair, from_odd_pair, yrecv, fresh_in, traced_in, fresh, traced):
    lane = lax.broadcasted_iota(jnp.int32, (LY, CZ), 1)
    place = lane % WIDTH
    even = is_even("sec")
    from_even, from_odd = from_even_pair[...], from_odd_pair[...]
    low = jnp.where(even, from_odd, from_even)
    high = jnp.where(even, from_even, from_odd)
    fields = []
    for comp in range(4):
        before = pltpu.roll(low, (CZ - 4 * comp) % CZ, 1)
        after = pltpu.roll(high, (CZ + 10 - 4 * comp) % CZ, 1)
        own = strip[comp]
        own = jnp.where(place < 2, before, own)
        fields.append(jnp.where((place == 12) | (place == 13), after, own))
    c = fields[:3]
    new = advance(c, fields[3], [both_ways(c, WIDTH, 1), both_ways(c, 1, 0), both_ways(c, 1, 1)])

    column = lax.broadcasted_iota(jnp.int32, (CY, CZ), 1)
    for i in range(3):
        part = new[i][:CY]
        for x in range(CX):
            first = WIDTH * (x + 2)
            left = pltpu.roll(part, (CZ - first - 2) % CZ, 1)
            right = pltpu.roll(part, (2 * CZ - 1 - first - 11) % CZ, 1)
            value = jnp.where(column == CZ - 1, right, fresh_in[i, x])
            fresh[i, x] = jnp.where(column == 0, left, value)

    outside = outside_walls()
    near = {}
    for i in range(3):
        a = jnp.where(outside, 0.0, new[i])
        for dz, field in enumerate((pltpu.roll(a, 1, 1), a, pltpu.roll(a, CZ - 1, 1))):
            shifts = (pltpu.roll(field, 1, 0), field, pltpu.roll(field, LY - 1, 0))
            for dy, shifted in enumerate(shifts):
                part = shifted[:CY]
                near[i, 0, dy, dz] = pltpu.roll(part, WIDTH, 1)
                near[i, 1, dy, dz] = part
                near[i, 2, dy, dz] = pltpu.roll(part, CZ - WIDTH, 1)
    moved = runge_kutta(lambda *key: near[key])

    rows = lax.broadcasted_iota(jnp.int32, (CY, CZ), 0)
    for slot in range(SLOTS):
        sx, sy, sz, steps = points_of(yrecv, slot)
        here = (rows == sy) & (steps > 0) & at_edge(sz)
        offset = jnp.where(sz < 2, sz + 2, sz - (CZ - 2) + 10)
        index = jnp.where(at_edge(sz), WIDTH * (sx + 2) + offset, 0)
        index = jnp.broadcast_to(index, (8, CZ))
        for i in range(3):
            got = jnp.concatenate([lanes_of(moved[i][8 * k : 8 * k + 8], index) for k in range(2)], 0)
            value = jnp.sum(jnp.where(here, got, 0.0), 0, keepdims=True)
            traced[i, slot : slot + 1, :] = traced_in[i, slot : slot + 1, :] + value


def shards(velocity, viscosity, counts, destination, seeds, substeps):
    def swap(value, axis, kept):
        n = lax.axis_size(axis)
        pairs = [(i, (i + 1) % n) for i in range(n) if kept(i)]
        return lax.ppermute(value, axis, pairs + [(b, a) for a, b in pairs])

    def exchange_x(even, odd):
        early = swap(even, "wide", lambda i: i % 2 == 0 and i % RUN < RUN // 2)
        odd = swap(odd, "wide", lambda i: i % 2 == 1)
        late = swap(even, "wide", lambda i: i % 2 == 0 and i % RUN >= RUN // 2)
        return early, late, odd

    def exchange_z(message):
        even = swap(message, "sec", lambda i: i % 2 == 0)
        return even, swap(message, "sec", lambda i: i % 2 == 1)

    message = shape(7, CY, CZ)
    own = jnp.concatenate([velocity.reshape(3 * CX, CY, CZ), viscosity], 0)
    x_odd, x_even = call(x_kernel, (message, message), [VMEM])(own)
    from_x = exchange_x(x_even, x_odd)
    base = call(
        points_kernel, shape(TILES, ROWS, CZ), [SMEM] + [VMEM] * 4, flops=1 << 20, moved=1 << 20
    )(
        destination.reshape(BLOCKS),
        counts,
        jnp.swapaxes(seeds.reshape(BLOCKS, 3, CZ), 0, 1),
        substeps.reshape(BLOCKS, CZ),
        own,
    )
    ymsg = call(y_kernel, shape(TILES, ROWS, CZ), [VMEM] * 4)(base, *from_x)
    yrecv = lax.all_to_all(ymsg, "tile", split_axis=0, concat_axis=0, tiled=True)
    zpart = call(z_kernel, shape(CY, CZ), [VMEM] * 4, flops=1 << 20, moved=1 << 20)(own, *from_x)
    edges, zmsg = call(
        edge_rows_kernel, (shape(N_ALL, 8, CZ), shape(LY, CZ)), [VMEM] * 2
    )(yrecv, zpart)
    from_z = exchange_z(zmsg)
    fresh, traced, strip = call(
        main_kernel,
        (shape(3, CX, CY, CZ), shape(3, SLOTS, CZ), shape(4, LY, CZ)),
        [VMEM] * 6,
        [
            pltpu.VMEM((N_ALL, LY, CZ), f32),
            pltpu.VMEM((CX + 2, 3, 3, 3, CY, CZ), f32),
            pltpu.VMEM((3, CX * CY, CZ), f32),
        ],
        flops=1 << 22,
        moved=1 << 23,
    )(own, *from_x, edges, yrecv)
    fresh, traced = call(
        strip_kernel, (shape(3, CX, CY, CZ), shape(3, SLOTS, CZ)), [VMEM] * 6
    )(strip, *from_z, yrecv, fresh, traced)
    return fresh, jnp.swapaxes(traced, 0, 1)[None, None, None]


def solution(mesh):
    in_specs = (
        P(None, "wide", "tile", "sec"),
        P("wide", "tile", "sec"),
        P("wide", "sec", "tile"),
        P("wide", "sec", "tile", None),
        P("wide", "sec", "tile", None, None, None),
        P("wide", "sec", "tile", None, None),
    )
    out_specs = (P(None, "wide", "tile", "sec"), P("wide", "sec", "tile", None, None, None))

    return jax.shard_map(shards, mesh=mesh, in_specs=in_specs, out_specs=out_specs, check_vma=False)
```

```python
import jax
import jax.numpy as jnp
from jax import lax
from jax.experimental import pallas as pl
from jax.experimental.pallas import tpu as pltpu
from jax.sharding import PartitionSpec as P


CAP = 2
CX, CY, CZ = 4, 16, 128
TILES = 4
BLOCKS = 4
SLOTS = TILES * CAP
LX = CX + 4
LY = 24
N_VEL = 3 * LX
N_ALL = N_VEL + CX + 2
HALO_ROWS = 26
PT_ROW = 56
ROWS = 64
WIDTH = CZ // LX
RUN = 8

flow_step = 0.2
trace_step = 1.25

VMEM = pl.BlockSpec(memory_space=pltpu.VMEM)
SMEM = pl.BlockSpec(memory_space=pltpu.SMEM)
f32 = jnp.float32


def call(kernel, out_shape, in_specs, scratch=(), flops=0, moved=0):
    return pl.pallas_call(
        kernel,
        out_shape=out_shape,
        in_specs=in_specs,
        out_specs=jax.tree.map(lambda _: VMEM, out_shape),
        scratch_shapes=list(scratch),
        compiler_params=pltpu.CompilerParams(vmem_limit_bytes=8 << 20),
        cost_estimate=pl.CostEstimate(flops=flops, bytes_accessed=moved, transcendentals=0),
    )


def shape(*dims):
    return jax.ShapeDtypeStruct(dims, f32)


def group_of(group):
    if group < N_VEL:
        return divmod(group, LX)
    return 3, group - N_VEL + 1


def is_even(axis):
    return lax.axis_index(axis) % 2 == 0


def of_even_pair(axis, early, late):
    return jnp.where(lax.axis_index(axis) % RUN < RUN // 2, early, late)


def plane_rows(group, first, size, own, early, late, odd):
    comp, x = group_of(group)
    rows = slice(first, first + size)
    if 2 <= x < 2 + CX:
        return own[CX * comp + x - 2, rows, :]
    index = 6 if comp == 3 else 2 * comp + x % 2
    from_odd = is_even("wide") if x < 2 else ~is_even("wide")
    even = of_even_pair("wide", early[index, rows, :], late[index, rows, :])
    return jnp.where(from_odd, odd[index, rows, :], even)


def inner(group):
    return 2 <= group_of(group)[1] < 2 + CX


def halo_rows(group):
    kind = [g for g in range(N_ALL) if inner(g) == inner(group)]
    first = HALO_ROWS if inner(group) else 0
    vels = [g for g in kind if g < N_VEL]
    if group < N_VEL:
        return first + 2 * kind.index(group), 2
    return first + len(vels) + kind.index(group), 1


def next_tiles():
    tile = lax.axis_index("tile")
    return (tile + 1) % TILES, (tile + TILES - 1) % TILES


def x_kernel(own, odd_first, even_first):
    even = is_even("wide")
    for c in range(4):
        for k in range(2 if c < 3 else 1):
            high = own[CX * c + (CX - 2 + k if c < 3 else CX - 1)]
            low = own[CX * c + k]
            odd_first[2 * c + k] = jnp.where(even, low, high)
            even_first[2 * c + k] = jnp.where(even, high, low)


def points_kernel(dest, counts, seeds, substeps, own, out):
    total = jnp.broadcast_to(counts[0], (4, CZ))
    live = [b < total for b in range(BLOCKS)]
    ranks = []
    for b in range(BLOCKS):
        rank = jnp.int32(0)
        for a in range(b):
            rank = rank + jnp.where(dest[a] == dest[b], 1, 0)
        ranks.append(rank)
    payload = [
        jnp.concatenate([seeds[c, b : b + 1, :] for c in range(3)] + [substeps[b : b + 1, :]], 0)
        for b in range(BLOCKS)
    ]
    for d in range(TILES):
        for r in range(CAP):
            slot = jnp.zeros((4, CZ), jnp.int32)
            for b in range(BLOCKS):
                chosen = live[b] & (dest[b] == d) & (ranks[b] == r)
                slot = jnp.where(chosen, payload[b], slot)
            out[d, PT_ROW + 4 * r : PT_ROW + 4 * r + 4, :] = slot.astype(f32)
    up, down = next_tiles()
    for g in range(N_ALL):
        if inner(g):
            row, n = halo_rows(g)
            out[up, row : row + n, :] = plane_rows(g, CY - n, n, own, None, None, None)
            out[down, row : row + n, :] = plane_rows(g, 0, n, own, None, None, None)


def y_kernel(base, early, late, odd, out):
    out[...] = base[...]
    up, down = next_tiles()
    for g in range(N_ALL):
        if not inner(g):
            row, n = halo_rows(g)
            out[up, row : row + n, :] = plane_rows(g, CY - n, n, None, early, late, odd)
            out[down, row : row + n, :] = plane_rows(g, 0, n, None, early, late, odd)


def columns(part, group, lane, acc):
    comp, x = group_of(group)
    place = WIDTH * x + 4 * comp
    moved = pltpu.roll(part, (place + 2) % CZ, 1)
    return jnp.where((lane >= place) & (lane < place + 4), moved, acc)


def z_kernel(own, early, late, odd, out):
    lane = lax.broadcasted_iota(jnp.int32, (CY, CZ), 1)
    acc = jnp.zeros((CY, CZ), f32)
    for g in range(N_ALL):
        acc = columns(plane_rows(g, 0, CY, own, early, late, odd), g, lane, acc)
    out[...] = acc


def edge_rows_kernel(yrecv, zpart, edges, z_even, z_odd):
    tile = lax.axis_index("tile")
    below = jnp.maximum(tile - 1, 0)
    above = jnp.minimum(tile + 1, TILES - 1)
    lane = lax.broadcasted_iota(jnp.int32, (8, CZ), 1)
    acc = jnp.zeros((8, CZ), f32)
    for g in range(N_ALL):
        row, n = halo_rows(g)
        high = jnp.where(tile < TILES - 1, yrecv[above, row : row + n, :], 0.0)
        low = jnp.where(tile > 0, yrecv[below, row : row + n, :], 0.0)
        edge = jnp.concatenate([high, jnp.zeros((8 - 2 * n, CZ), f32), low], 0)
        edges[g] = edge
        acc = columns(edge, g, lane, acc)
    for message in (z_even, z_odd):
        message[0:CY, :] = zpart[...]
        message[CY:LY, :] = acc


def outside_walls():
    tile = lax.axis_index("tile")
    row = lax.broadcasted_iota(jnp.int32, (LY, CZ), 0)
    return ((tile == 0) & (row == LY - 1)) | ((tile == TILES - 1) & (row == CY))


def flux(one, two, d):
    both = one[d] + two[d]
    return [0.25 * (one[i] + two[i]) * both for i in range(3)]


def advance(c, viscous, sides):
    spread = [0.0] * 3
    laplace = [0.0] * 3
    for d, (lower, upper) in enumerate(sides):
        f_up, f_down = flux(c, upper, d), flux(lower, c, d)
        spread = [spread[i] + (f_up[i] - f_down[i]) for i in range(3)]
        laplace = [laplace[i] + (upper[i] + lower[i]) for i in range(3)]
    return [
        c[i] + flow_step * (viscous * (laplace[i] - 6.0 * c[i]) - spread[i]) for i in range(3)
    ]


def both_ways(fields, step, axis):
    n = fields[0].shape[axis]
    return (
        [pltpu.roll(v, step, axis) for v in fields],
        [pltpu.roll(v, n - step, axis) for v in fields],
    )


def runge_kutta(near):
    def sample(e):
        weights = [(jnp.maximum(-v, 0.0), 1.0 - jnp.abs(v), jnp.maximum(v, 0.0)) for v in e]
        total = [0.0] * 3
        for dx in range(3):
            plane = [0.0] * 3
            for dy in range(3):
                for i in range(3):
                    line = sum(weights[2][dz] * near(i, dx, dy, dz) for dz in range(3))
                    plane[i] = plane[i] + weights[1][dy] * line
            total = [total[i] + weights[0][dx] * plane[i] for i in range(3)]
        return total

    k1 = [near(i, 1, 1, 1) for i in range(3)]
    k2 = sample([(0.5 * trace_step) * v for v in k1])
    k3 = sample([(0.5 * trace_step) * v for v in k2])
    k4 = sample([trace_step * v for v in k3])
    return [
        (trace_step / 6.0) * (k1[i] + 2.0 * k2[i] + 2.0 * k3[i] + k4[i]) for i in range(3)
    ]


def points_of(yrecv, slot):
    s, r = divmod(slot, CAP)
    rows = yrecv[s, PT_ROW + 4 * r : PT_ROW + 4 * r + 4, :].astype(jnp.int32)
    return [rows[k : k + 1] for k in range(4)]


def at_edge(z):
    return (z < 2) | (z >= CZ - 2)


def lanes_of(table, index):
    return jnp.take_along_axis(table, index, axis=1, mode="promise_in_bounds")


def main_kernel(own, early, late, odd, edges, yrecv, fresh, traced, strip, whole, near, table):
    lane = lax.broadcasted_iota(jnp.int32, (LY, CZ), 1)
    strips = [jnp.zeros((LY, CZ), f32) for _ in range(4)]
    for g in range(N_ALL):
        comp, x = group_of(g)
        whole[g, 0:CY, :] = plane_rows(g, 0, CY, own, early, late, odd)
        whole[g, CY:LY, :] = edges[g]
        plane = whole[g]
        place = WIDTH * x
        start_columns = pltpu.roll(plane, (place + 2) % CZ, 1)
        end_columns = pltpu.roll(plane, (place + 12) % CZ, 1)
        acc = jnp.where((lane >= place + 2) & (lane < place + 6), start_columns, strips[comp])
        strips[comp] = jnp.where((lane >= place + 8) & (lane < place + 12), end_columns, acc)
    for comp in range(4):
        strip[comp] = strips[comp]

    outside = outside_walls()
    for x in range(CX + 2):
        c = [whole[i * LX + x + 1] for i in range(3)]
        sides = [
            ([whole[i * LX + x] for i in range(3)], [whole[i * LX + x + 2] for i in range(3)]),
            both_ways(c, 1, 0),
            both_ways(c, 1, 1),
        ]
        new = advance(c, whole[N_VEL + x], sides)
        for i in range(3):
            if 1 <= x <= CX:
                fresh[i, x - 1] = new[i][:CY]
            a = jnp.where(outside, 0.0, new[i])
            for dz, field in enumerate((pltpu.roll(a, 1, 1), a, pltpu.roll(a, CZ - 1, 1))):
                near[x, i, 0, dz] = pltpu.roll(field, 1, 0)[:CY]
                near[x, i, 1, dz] = field[:CY]
                near[x, i, 2, dz] = pltpu.roll(field, LY - 1, 0)[:CY]

    for x in range(CX):
        moved = runge_kutta(lambda i, dx, dy, dz: near[x + dx, i, dy, dz])
        for i in range(3):
            table[i, x * CY : (x + 1) * CY, :] = moved[i]

    rows = lax.broadcasted_iota(jnp.int32, (CX * CY, CZ), 0)
    for slot in range(SLOTS):
        sx, sy, sz, steps = points_of(yrecv, slot)
        here = (rows == sx * CY + sy) & (steps > 0) & ~at_edge(sz)
        index = jnp.broadcast_to(sz, (8, CZ))
        for i in range(3):
            got = jnp.concatenate(
                [lanes_of(table[i, 8 * k : 8 * k + 8, :], index) for k in range(CX * CY // 8)], 0
            )
            traced[i, slot : slot + 1, :] = jnp.sum(jnp.where(here, got, 0.0), 0, keepdims=True)


def strip_kernel(strip, early, late, odd, yrecv, fresh_in, traced_in, fresh, traced):
    lane = lax.broadcasted_iota(jnp.int32, (LY, CZ), 1)
    place = lane % WIDTH
    even = is_even("sec")
    from_odd, from_even = odd[...], of_even_pair("sec", early[...], late[...])
    low = jnp.where(even, from_odd, from_even)
    high = jnp.where(even, from_even, from_odd)
    fields = []
    for comp in range(4):
        before = pltpu.roll(low, (CZ - 4 * comp) % CZ, 1)
        after = pltpu.roll(high, (CZ + 10 - 4 * comp) % CZ, 1)
        own = strip[comp]
        own = jnp.where(place < 2, before, own)
        fields.append(jnp.where((place == 12) | (place == 13), after, own))
    c = fields[:3]
    new = advance(c, fields[3], [both_ways(c, WIDTH, 1), both_ways(c, 1, 0), both_ways(c, 1, 1)])

    column = lax.broadcasted_iota(jnp.int32, (CY, CZ), 1)
    for i in range(3):
        part = new[i][:CY]
        for x in range(CX):
            first = WIDTH * (x + 2)
            left = pltpu.roll(part, (CZ - first - 2) % CZ, 1)
            right = pltpu.roll(part, (2 * CZ - 1 - first - 11) % CZ, 1)
            value = jnp.where(column == CZ - 1, right, fresh_in[i, x])
            fresh[i, x] = jnp.where(column == 0, left, value)

    outside = outside_walls()
    near = {}
    for i in range(3):
        a = jnp.where(outside, 0.0, new[i])
        for dz, field in enumerate((pltpu.roll(a, 1, 1), a, pltpu.roll(a, CZ - 1, 1))):
            shifts = (pltpu.roll(field, 1, 0), field, pltpu.roll(field, LY - 1, 0))
            for dy, shifted in enumerate(shifts):
                part = shifted[:CY]
                near[i, 0, dy, dz] = pltpu.roll(part, WIDTH, 1)
                near[i, 1, dy, dz] = part
                near[i, 2, dy, dz] = pltpu.roll(part, CZ - WIDTH, 1)
    moved = runge_kutta(lambda *key: near[key])

    rows = lax.broadcasted_iota(jnp.int32, (CY, CZ), 0)
    for slot in range(SLOTS):
        sx, sy, sz, steps = points_of(yrecv, slot)
        here = (rows == sy) & (steps > 0) & at_edge(sz)
        offset = jnp.where(sz < 2, sz + 2, sz - (CZ - 2) + 10)
        index = jnp.where(at_edge(sz), WIDTH * (sx + 2) + offset, 0)
        index = jnp.broadcast_to(index, (8, CZ))
        for i in range(3):
            got = jnp.concatenate([lanes_of(moved[i][8 * k : 8 * k + 8], index) for k in range(2)], 0)
            value = jnp.sum(jnp.where(here, got, 0.0), 0, keepdims=True)
            traced[i, slot : slot + 1, :] = traced_in[i, slot : slot + 1, :] + value


def shards(velocity, viscosity, counts, destination, seeds, substeps):
    def swap(value, axis, kept):
        n = lax.axis_size(axis)
        pairs = [(i, (i + 1) % n) for i in range(n) if kept(i)]
        return lax.ppermute(value, axis, pairs + [(b, a) for a, b in pairs])

    def exchange(even, odd, axis):
        early = swap(even, axis, lambda i: i % 2 == 0 and i % RUN < RUN // 2)
        odd = swap(odd, axis, lambda i: i % 2 == 1)
        late = swap(even, axis, lambda i: i % 2 == 0 and i % RUN >= RUN // 2)
        return early, late, odd

    message = shape(7, CY, CZ)
    own = jnp.concatenate([velocity.reshape(3 * CX, CY, CZ), viscosity], 0)
    x_odd, x_even = call(x_kernel, (message, message), [VMEM])(own)
    from_x = exchange(x_even, x_odd, "wide")
    base = call(
        points_kernel, shape(TILES, ROWS, CZ), [SMEM] + [VMEM] * 4, flops=1 << 20, moved=1 << 20
    )(
        destination.reshape(BLOCKS),
        counts,
        jnp.swapaxes(seeds.reshape(BLOCKS, 3, CZ), 0, 1),
        substeps.reshape(BLOCKS, CZ),
        own,
    )
    ymsg = call(y_kernel, shape(TILES, ROWS, CZ), [VMEM] * 4)(base, *from_x)
    yrecv = lax.all_to_all(ymsg, "tile", split_axis=0, concat_axis=0, tiled=True)
    zpart = call(z_kernel, shape(CY, CZ), [VMEM] * 4, flops=1 << 20, moved=1 << 20)(own, *from_x)
    edges, z_even, z_odd = call(
        edge_rows_kernel, (shape(N_ALL, 8, CZ), shape(LY, CZ), shape(LY, CZ)), [VMEM] * 2
    )(yrecv, zpart)
    from_z = exchange(z_even, z_odd, "sec")
    fresh, traced, strip = call(
        main_kernel,
        (shape(3, CX, CY, CZ), shape(3, SLOTS, CZ), shape(4, LY, CZ)),
        [VMEM] * 6,
        [
            pltpu.VMEM((N_ALL, LY, CZ), f32),
            pltpu.VMEM((CX + 2, 3, 3, 3, CY, CZ), f32),
            pltpu.VMEM((3, CX * CY, CZ), f32),
        ],
        flops=1 << 22,
        moved=1 << 23,
    )(own, *from_x, edges, yrecv)
    fresh, traced = call(
        strip_kernel, (shape(3, CX, CY, CZ), shape(3, SLOTS, CZ)), [VMEM] * 7
    )(strip, *from_z, yrecv, fresh, traced)
    return fresh, jnp.swapaxes(traced, 0, 1)[None, None, None]


def solution(mesh):
    in_specs = (
        P(None, "wide", "tile", "sec"),
        P("wide", "tile", "sec"),
        P("wide", "sec", "tile"),
        P("wide", "sec", "tile", None),
        P("wide", "sec", "tile", None, None, None),
        P("wide", "sec", "tile", None, None),
    )
    out_specs = (P(None, "wide", "tile", "sec"), P("wide", "sec", "tile", None, None, None))

    return jax.shard_map(shards, mesh=mesh, in_specs=in_specs, out_specs=out_specs, check_vma=False)
```

```python
import jax
import jax.numpy as jnp
from jax import lax
from jax.experimental import pallas as pl
from jax.experimental.pallas import tpu as pltpu
from jax.sharding import PartitionSpec as P


CAP = 2
CX, CY, CZ = 4, 16, 128
TILES = 4
BLOCKS = 4
SLOTS = TILES * CAP
LX = CX + 4
LY = 24
N_VEL = 3 * LX
N_ALL = N_VEL + CX + 2
HALO_ROWS = 26
PT_ROW = 56
ROWS = 64
WIDTH = CZ // LX
RUN = 8

flow_step = 0.2
trace_step = 1.25

VMEM = pl.BlockSpec(memory_space=pltpu.VMEM)
SMEM = pl.BlockSpec(memory_space=pltpu.SMEM)
f32 = jnp.float32


def call(kernel, out_shape, in_specs, scratch=(), flops=0, moved=0):
    return pl.pallas_call(
        kernel,
        out_shape=out_shape,
        in_specs=in_specs,
        out_specs=jax.tree.map(lambda _: VMEM, out_shape),
        scratch_shapes=list(scratch),
        compiler_params=pltpu.CompilerParams(vmem_limit_bytes=8 << 20),
        cost_estimate=pl.CostEstimate(flops=flops, bytes_accessed=moved, transcendentals=0),
    )


def shape(*dims):
    return jax.ShapeDtypeStruct(dims, f32)


def group_of(group):
    if group < N_VEL:
        return divmod(group, LX)
    return 3, group - N_VEL + 1


def is_even(axis):
    return lax.axis_index(axis) % 2 == 0


def of_even_pair(axis, early, late):
    return jnp.where(lax.axis_index(axis) % RUN < RUN // 2, early, late)


def plane_rows(group, first, size, own, early, late, odd):
    comp, x = group_of(group)
    rows = slice(first, first + size)
    if 2 <= x < 2 + CX:
        return own[CX * comp + x - 2, rows, :]
    index = 6 if comp == 3 else 2 * comp + x % 2
    from_odd = is_even("wide") if x < 2 else ~is_even("wide")
    even = of_even_pair("wide", early[index, rows, :], late[index, rows, :])
    return jnp.where(from_odd, odd[index, rows, :], even)


def inner(group):
    return 2 <= group_of(group)[1] < 2 + CX


def halo_rows(group):
    kind = [g for g in range(N_ALL) if inner(g) == inner(group)]
    first = HALO_ROWS if inner(group) else 0
    vels = [g for g in kind if g < N_VEL]
    if group < N_VEL:
        return first + 2 * kind.index(group), 2
    return first + len(vels) + kind.index(group), 1


def next_tiles():
    tile = lax.axis_index("tile")
    return (tile + 1) % TILES, (tile + TILES - 1) % TILES


def x_kernel(own, odd_first, even_first):
    even = is_even("wide")
    for c in range(4):
        for k in range(2 if c < 3 else 1):
            high = own[CX * c + (CX - 2 + k if c < 3 else CX - 1)]
            low = own[CX * c + k]
            odd_first[2 * c + k] = jnp.where(even, low, high)
            even_first[2 * c + k] = jnp.where(even, high, low)


def points_kernel(dest, counts, seeds, substeps, own, out):
    total = jnp.broadcast_to(counts[0], (4, CZ))
    live = [b < total for b in range(BLOCKS)]
    ranks = []
    for b in range(BLOCKS):
        rank = jnp.int32(0)
        for a in range(b):
            rank = rank + jnp.where(dest[a] == dest[b], 1, 0)
        ranks.append(rank)
    payload = [
        jnp.concatenate([seeds[c, b : b + 1, :] for c in range(3)] + [substeps[b : b + 1, :]], 0)
        for b in range(BLOCKS)
    ]
    for d in range(TILES):
        for r in range(CAP):
            slot = jnp.zeros((4, CZ), jnp.int32)
            for b in range(BLOCKS):
                chosen = live[b] & (dest[b] == d) & (ranks[b] == r)
                slot = jnp.where(chosen, payload[b], slot)
            out[d, PT_ROW + 4 * r : PT_ROW + 4 * r + 4, :] = slot.astype(f32)
    up, down = next_tiles()
    for g in range(N_ALL):
        if inner(g):
            row, n = halo_rows(g)
            out[up, row : row + n, :] = plane_rows(g, CY - n, n, own, None, None, None)
            out[down, row : row + n, :] = plane_rows(g, 0, n, own, None, None, None)


def y_kernel(base, early, late, odd, by_3, by_1, by_2, mine, out):
    out[...] = base[...]
    up, down = next_tiles()
    for g in range(N_ALL):
        if not inner(g):
            row, n = halo_rows(g)
            out[up, row : row + n, :] = plane_rows(g, CY - n, n, None, early, late, odd)
            out[down, row : row + n, :] = plane_rows(g, 0, n, None, early, late, odd)
    tile = lax.axis_index("tile")
    by_3[...] = out[TILES - 1 - tile]
    by_1[...] = out[tile + 1 - 2 * (tile % 2)]
    by_2[...] = out[(tile + 2) % TILES, PT_ROW:ROWS, :]
    mine[...] = out[tile, PT_ROW:ROWS, :]


def columns(part, group, lane, acc):
    comp, x = group_of(group)
    place = WIDTH * x + 4 * comp
    moved = pltpu.roll(part, (place + 2) % CZ, 1)
    return jnp.where((lane >= place) & (lane < place + 4), moved, acc)


def z_kernel(own, early, late, odd, out):
    lane = lax.broadcasted_iota(jnp.int32, (CY, CZ), 1)
    acc = jnp.zeros((CY, CZ), f32)
    for g in range(N_ALL):
        acc = columns(plane_rows(g, 0, CY, own, early, late, odd), g, lane, acc)
    out[...] = acc


def edge_rows_kernel(by_3, by_1, zpart, edges, z_even, z_odd):
    tile = lax.axis_index("tile")
    even = is_even("tile")
    lane = lax.broadcasted_iota(jnp.int32, (8, CZ), 1)
    acc = jnp.zeros((8, CZ), f32)
    for g in range(N_ALL):
        row, n = halo_rows(g)
        near, far = by_1[row : row + n, :], by_3[row : row + n, :]
        high = jnp.where(tile < TILES - 1, jnp.where(even, near, far), 0.0)
        low = jnp.where(tile > 0, jnp.where(even, far, near), 0.0)
        edge = jnp.concatenate([high, jnp.zeros((8 - 2 * n, CZ), f32), low], 0)
        edges[g] = edge
        acc = columns(edge, g, lane, acc)
    for message in (z_even, z_odd):
        message[0:CY, :] = zpart[...]
        message[CY:LY, :] = acc


def outside_walls():
    tile = lax.axis_index("tile")
    row = lax.broadcasted_iota(jnp.int32, (LY, CZ), 0)
    return ((tile == 0) & (row == LY - 1)) | ((tile == TILES - 1) & (row == CY))


def flux(one, two, d):
    both = one[d] + two[d]
    return [0.25 * (one[i] + two[i]) * both for i in range(3)]


def advance(c, viscous, sides):
    spread = [0.0] * 3
    laplace = [0.0] * 3
    for d, (lower, upper) in enumerate(sides):
        f_up, f_down = flux(c, upper, d), flux(lower, c, d)
        spread = [spread[i] + (f_up[i] - f_down[i]) for i in range(3)]
        laplace = [laplace[i] + (upper[i] + lower[i]) for i in range(3)]
    return [
        c[i] + flow_step * (viscous * (laplace[i] - 6.0 * c[i]) - spread[i]) for i in range(3)
    ]


def both_ways(fields, step, axis):
    n = fields[0].shape[axis]
    return (
        [pltpu.roll(v, step, axis) for v in fields],
        [pltpu.roll(v, n - step, axis) for v in fields],
    )


def runge_kutta(near):
    def sample(e):
        weights = [(jnp.maximum(-v, 0.0), 1.0 - jnp.abs(v), jnp.maximum(v, 0.0)) for v in e]
        total = [0.0] * 3
        for dx in range(3):
            plane = [0.0] * 3
            for dy in range(3):
                for i in range(3):
                    line = sum(weights[2][dz] * near(i, dx, dy, dz) for dz in range(3))
                    plane[i] = plane[i] + weights[1][dy] * line
            total = [total[i] + weights[0][dx] * plane[i] for i in range(3)]
        return total

    k1 = [near(i, 1, 1, 1) for i in range(3)]
    k2 = sample([(0.5 * trace_step) * v for v in k1])
    k3 = sample([(0.5 * trace_step) * v for v in k2])
    k4 = sample([trace_step * v for v in k3])
    return [
        (trace_step / 6.0) * (k1[i] + 2.0 * k2[i] + 2.0 * k3[i] + k4[i]) for i in range(3)
    ]


def points_of(points, slot):
    s, r = divmod(slot, CAP)
    rows = points[s, 4 * r : 4 * r + 4, :].astype(jnp.int32)
    return [rows[k : k + 1] for k in range(4)]


def at_edge(z):
    return (z < 2) | (z >= CZ - 2)


def lanes_of(table, index):
    return jnp.take_along_axis(table, index, axis=1, mode="promise_in_bounds")


def main_kernel(
    own, early, late, odd, edges, by_3, by_1, by_2, mine, fresh, traced, strip, points, whole, near, table
):
    tile = lax.axis_index("tile")
    for s in range(TILES):
        part = jnp.where(tile == TILES - 1 - s, by_3[PT_ROW:ROWS, :], mine[...])
        part = jnp.where(tile == s + 1 - 2 * (s % 2), by_1[PT_ROW:ROWS, :], part)
        points[s] = jnp.where(tile == (s + 2) % TILES, by_2[...], part)
    lane = lax.broadcasted_iota(jnp.int32, (LY, CZ), 1)
    strips = [jnp.zeros((LY, CZ), f32) for _ in range(4)]
    for g in range(N_ALL):
        comp, x = group_of(g)
        whole[g, 0:CY, :] = plane_rows(g, 0, CY, own, early, late, odd)
        whole[g, CY:LY, :] = edges[g]
        plane = whole[g]
        place = WIDTH * x
        start_columns = pltpu.roll(plane, (place + 2) % CZ, 1)
        end_columns = pltpu.roll(plane, (place + 12) % CZ, 1)
        acc = jnp.where((lane >= place + 2) & (lane < place + 6), start_columns, strips[comp])
        strips[comp] = jnp.where((lane >= place + 8) & (lane < place + 12), end_columns, acc)
    for comp in range(4):
        strip[comp] = strips[comp]

    outside = outside_walls()
    for x in range(CX + 2):
        c = [whole[i * LX + x + 1] for i in range(3)]
        sides = [
            ([whole[i * LX + x] for i in range(3)], [whole[i * LX + x + 2] for i in range(3)]),
            both_ways(c, 1, 0),
            both_ways(c, 1, 1),
        ]
        new = advance(c, whole[N_VEL + x], sides)
        for i in range(3):
            if 1 <= x <= CX:
                fresh[i, x - 1] = new[i][:CY]
            a = jnp.where(outside, 0.0, new[i])
            for dz, field in enumerate((pltpu.roll(a, 1, 1), a, pltpu.roll(a, CZ - 1, 1))):
                near[x, i, 0, dz] = pltpu.roll(field, 1, 0)[:CY]
                near[x, i, 1, dz] = field[:CY]
                near[x, i, 2, dz] = pltpu.roll(field, LY - 1, 0)[:CY]

    for x in range(CX):
        moved = runge_kutta(lambda i, dx, dy, dz: near[x + dx, i, dy, dz])
        for i in range(3):
            table[i, x * CY : (x + 1) * CY, :] = moved[i]

    rows = lax.broadcasted_iota(jnp.int32, (CX * CY, CZ), 0)
    for slot in range(SLOTS):
        sx, sy, sz, steps = points_of(points, slot)
        here = (rows == sx * CY + sy) & (steps > 0) & ~at_edge(sz)
        index = jnp.broadcast_to(sz, (8, CZ))
        for i in range(3):
            got = jnp.concatenate(
                [lanes_of(table[i, 8 * k : 8 * k + 8, :], index) for k in range(CX * CY // 8)], 0
            )
            traced[i, slot : slot + 1, :] = jnp.sum(jnp.where(here, got, 0.0), 0, keepdims=True)


def strip_kernel(strip, early, late, odd, points, fresh_in, traced_in, fresh, traced):
    lane = lax.broadcasted_iota(jnp.int32, (LY, CZ), 1)
    place = lane % WIDTH
    even = is_even("sec")
    from_odd, from_even = odd[...], of_even_pair("sec", early[...], late[...])
    low = jnp.where(even, from_odd, from_even)
    high = jnp.where(even, from_even, from_odd)
    fields = []
    for comp in range(4):
        before = pltpu.roll(low, (CZ - 4 * comp) % CZ, 1)
        after = pltpu.roll(high, (CZ + 10 - 4 * comp) % CZ, 1)
        own = strip[comp]
        own = jnp.where(place < 2, before, own)
        fields.append(jnp.where((place == 12) | (place == 13), after, own))
    c = fields[:3]
    new = advance(c, fields[3], [both_ways(c, WIDTH, 1), both_ways(c, 1, 0), both_ways(c, 1, 1)])

    column = lax.broadcasted_iota(jnp.int32, (CY, CZ), 1)
    for i in range(3):
        part = new[i][:CY]
        for x in range(CX):
            first = WIDTH * (x + 2)
            left = pltpu.roll(part, (CZ - first - 2) % CZ, 1)
            right = pltpu.roll(part, (2 * CZ - 1 - first - 11) % CZ, 1)
            value = jnp.where(column == CZ - 1, right, fresh_in[i, x])
            fresh[i, x] = jnp.where(column == 0, left, value)

    outside = outside_walls()
    near = {}
    for i in range(3):
        a = jnp.where(outside, 0.0, new[i])
        for dz, field in enumerate((pltpu.roll(a, 1, 1), a, pltpu.roll(a, CZ - 1, 1))):
            shifts = (pltpu.roll(field, 1, 0), field, pltpu.roll(field, LY - 1, 0))
            for dy, shifted in enumerate(shifts):
                part = shifted[:CY]
                near[i, 0, dy, dz] = pltpu.roll(part, WIDTH, 1)
                near[i, 1, dy, dz] = part
                near[i, 2, dy, dz] = pltpu.roll(part, CZ - WIDTH, 1)
    moved = runge_kutta(lambda *key: near[key])

    rows = lax.broadcasted_iota(jnp.int32, (CY, CZ), 0)
    for slot in range(SLOTS):
        sx, sy, sz, steps = points_of(points, slot)
        here = (rows == sy) & (steps > 0) & at_edge(sz)
        offset = jnp.where(sz < 2, sz + 2, sz - (CZ - 2) + 10)
        index = jnp.where(at_edge(sz), WIDTH * (sx + 2) + offset, 0)
        index = jnp.broadcast_to(index, (8, CZ))
        for i in range(3):
            got = jnp.concatenate([lanes_of(moved[i][8 * k : 8 * k + 8], index) for k in range(2)], 0)
            value = jnp.sum(jnp.where(here, got, 0.0), 0, keepdims=True)
            traced[i, slot : slot + 1, :] = traced_in[i, slot : slot + 1, :] + value


def shards(velocity, viscosity, counts, destination, seeds, substeps):
    def swap(value, axis, kept):
        n = lax.axis_size(axis)
        pairs = [(i, (i + 1) % n) for i in range(n) if kept(i)]
        return lax.ppermute(value, axis, pairs + [(b, a) for a, b in pairs])

    def swap_tiles(value, k):
        return lax.ppermute(value, "tile", [(i, i ^ k) for i in range(TILES)])

    def exchange(even, odd, axis):
        early = swap(even, axis, lambda i: i % 2 == 0 and i % RUN < RUN // 2)
        odd = swap(odd, axis, lambda i: i % 2 == 1)
        late = swap(even, axis, lambda i: i % 2 == 0 and i % RUN >= RUN // 2)
        return early, late, odd

    message = shape(7, CY, CZ)
    own = jnp.concatenate([velocity.reshape(3 * CX, CY, CZ), viscosity], 0)
    x_odd, x_even = call(x_kernel, (message, message), [VMEM])(own)
    from_x = exchange(x_even, x_odd, "wide")
    base = call(
        points_kernel, shape(TILES, ROWS, CZ), [SMEM] + [VMEM] * 4, flops=1 << 20, moved=1 << 20
    )(
        destination.reshape(BLOCKS),
        counts,
        jnp.swapaxes(seeds.reshape(BLOCKS, 3, CZ), 0, 1),
        substeps.reshape(BLOCKS, CZ),
        own,
    )
    messages = (shape(ROWS, CZ), shape(ROWS, CZ), shape(ROWS - PT_ROW, CZ), shape(ROWS - PT_ROW, CZ))
    to_3, to_1, to_2, mine = call(
        y_kernel, messages, [VMEM] * 4, [pltpu.VMEM((TILES, ROWS, CZ), f32)]
    )(base, *from_x)
    by_3, by_1, by_2 = (
        swap_tiles(value, k) for value, k in ((to_3, 3), (to_1, 1), (to_2, 2))
    )
    zpart = call(z_kernel, shape(CY, CZ), [VMEM] * 4, flops=1 << 20, moved=1 << 20)(own, *from_x)
    edges, z_even, z_odd = call(
        edge_rows_kernel, (shape(N_ALL, 8, CZ), shape(LY, CZ), shape(LY, CZ)), [VMEM] * 3
    )(by_3, by_1, zpart)
    from_z = exchange(z_even, z_odd, "sec")
    fresh, traced, strip, points = call(
        main_kernel,
        (
            shape(3, CX, CY, CZ),
            shape(3, SLOTS, CZ),
            shape(4, LY, CZ),
            shape(TILES, ROWS - PT_ROW, CZ),
        ),
        [VMEM] * 9,
        [
            pltpu.VMEM((N_ALL, LY, CZ), f32),
            pltpu.VMEM((CX + 2, 3, 3, 3, CY, CZ), f32),
            pltpu.VMEM((3, CX * CY, CZ), f32),
        ],
        flops=1 << 22,
        moved=1 << 23,
    )(own, *from_x, edges, by_3, by_1, by_2, mine)
    fresh, traced = call(
        strip_kernel, (shape(3, CX, CY, CZ), shape(3, SLOTS, CZ)), [VMEM] * 7
    )(strip, *from_z, points, fresh, traced)
    return fresh, jnp.swapaxes(traced, 0, 1)[None, None, None]


def solution(mesh):
    in_specs = (
        P(None, "wide", "tile", "sec"),
        P("wide", "tile", "sec"),
        P("wide", "sec", "tile"),
        P("wide", "sec", "tile", None),
        P("wide", "sec", "tile", None, None, None),
        P("wide", "sec", "tile", None, None),
    )
    out_specs = (P(None, "wide", "tile", "sec"), P("wide", "sec", "tile", None, None, None))

    return jax.shard_map(shards, mesh=mesh, in_specs=in_specs, out_specs=out_specs, check_vma=False)
```

```python
import jax
import jax.numpy as jnp
from jax import lax
from jax.experimental import pallas as pl
from jax.experimental.pallas import tpu as pltpu
from jax.sharding import PartitionSpec as P


CAP = 2
CX, CY, CZ = 4, 16, 128
TILES = 4
BLOCKS = 4
SLOTS = TILES * CAP
LX = CX + 4
LY = 24
N_VEL = 3 * LX
N_ALL = N_VEL + CX + 2
HALO_ROWS = 26
PT_ROW = 56
ROWS = 64
WIDTH = CZ // LX
RUN = 8

flow_step = 0.2
trace_step = 1.25

VMEM = pl.BlockSpec(memory_space=pltpu.VMEM)
SMEM = pl.BlockSpec(memory_space=pltpu.SMEM)
f32 = jnp.float32


def call(kernel, out_shape, in_specs, scratch=(), flops=0, moved=0):
    return pl.pallas_call(
        kernel,
        out_shape=out_shape,
        in_specs=in_specs,
        out_specs=jax.tree.map(lambda _: VMEM, out_shape),
        scratch_shapes=list(scratch),
        compiler_params=pltpu.CompilerParams(vmem_limit_bytes=8 << 20),
        cost_estimate=pl.CostEstimate(flops=flops, bytes_accessed=moved, transcendentals=0),
    )


def shape(*dims):
    return jax.ShapeDtypeStruct(dims, f32)


def group_of(group):
    if group < N_VEL:
        return divmod(group, LX)
    return 3, group - N_VEL + 1


def is_even(axis):
    return lax.axis_index(axis) % 2 == 0


def of_even_pair(axis, early, late, span=RUN // 2):
    return jnp.where(lax.axis_index(axis) % RUN < span, early, late)


def plane_rows(group, first, size, own, early, late, odd):
    comp, x = group_of(group)
    rows = slice(first, first + size)
    if 2 <= x < 2 + CX:
        return own[CX * comp + x - 2, rows, :]
    index = 6 if comp == 3 else 2 * comp + x % 2
    from_odd = is_even("wide") if x < 2 else ~is_even("wide")
    even = of_even_pair("wide", early[index, rows, :], late[index, rows, :])
    return jnp.where(from_odd, odd[index, rows, :], even)


def inner(group):
    return 2 <= group_of(group)[1] < 2 + CX


def halo_rows(group):
    kind = [g for g in range(N_ALL) if inner(g) == inner(group)]
    first = HALO_ROWS if inner(group) else 0
    vels = [g for g in kind if g < N_VEL]
    if group < N_VEL:
        return first + 2 * kind.index(group), 2
    return first + len(vels) + kind.index(group), 1


def next_tiles():
    tile = lax.axis_index("tile")
    return (tile + 1) % TILES, (tile + TILES - 1) % TILES


def x_kernel(own, odd_first, even_first):
    even = is_even("wide")
    for c in range(4):
        for k in range(2 if c < 3 else 1):
            high = own[CX * c + (CX - 2 + k if c < 3 else CX - 1)]
            low = own[CX * c + k]
            odd_first[2 * c + k] = jnp.where(even, low, high)
            even_first[2 * c + k] = jnp.where(even, high, low)


def points_kernel(dest, counts, seeds, substeps, own, out):
    total = jnp.broadcast_to(counts[0], (4, CZ))
    live = [b < total for b in range(BLOCKS)]
    ranks = []
    for b in range(BLOCKS):
        rank = jnp.int32(0)
        for a in range(b):
            rank = rank + jnp.where(dest[a] == dest[b], 1, 0)
        ranks.append(rank)
    payload = [
        jnp.concatenate([seeds[c, b : b + 1, :] for c in range(3)] + [substeps[b : b + 1, :]], 0)
        for b in range(BLOCKS)
    ]
    for d in range(TILES):
        for r in range(CAP):
            slot = jnp.zeros((4, CZ), jnp.int32)
            for b in range(BLOCKS):
                chosen = live[b] & (dest[b] == d) & (ranks[b] == r)
                slot = jnp.where(chosen, payload[b], slot)
            out[d, PT_ROW + 4 * r : PT_ROW + 4 * r + 4, :] = slot.astype(f32)
    up, down = next_tiles()
    for g in range(N_ALL):
        if inner(g):
            row, n = halo_rows(g)
            out[up, row : row + n, :] = plane_rows(g, CY - n, n, own, None, None, None)
            out[down, row : row + n, :] = plane_rows(g, 0, n, own, None, None, None)


def y_kernel(base, early, late, odd, by_3, by_1, by_2, mine, out):
    out[...] = base[...]
    up, down = next_tiles()
    for g in range(N_ALL):
        if not inner(g):
            row, n = halo_rows(g)
            out[up, row : row + n, :] = plane_rows(g, CY - n, n, None, early, late, odd)
            out[down, row : row + n, :] = plane_rows(g, 0, n, None, early, late, odd)
    tile = lax.axis_index("tile")
    by_3[...] = out[TILES - 1 - tile]
    by_1[...] = out[tile + 1 - 2 * (tile % 2)]
    by_2[...] = out[(tile + 2) % TILES, PT_ROW:ROWS, :]
    mine[...] = out[tile, PT_ROW:ROWS, :]


def columns(part, group, lane, acc):
    comp, x = group_of(group)
    place = WIDTH * x + 4 * comp
    moved = pltpu.roll(part, (place + 2) % CZ, 1)
    return jnp.where((lane >= place) & (lane < place + 4), moved, acc)


def z_kernel(own, early, late, odd, out):
    lane = lax.broadcasted_iota(jnp.int32, (CY, CZ), 1)
    acc = jnp.zeros((CY, CZ), f32)
    for g in range(N_ALL):
        acc = columns(plane_rows(g, 0, CY, own, early, late, odd), g, lane, acc)
    out[...] = acc


def edge_rows_kernel(by_3, by_1, zpart, edges, z_even, z_odd):
    tile = lax.axis_index("tile")
    even = is_even("tile")
    lane = lax.broadcasted_iota(jnp.int32, (8, CZ), 1)
    acc = jnp.zeros((8, CZ), f32)
    for g in range(N_ALL):
        row, n = halo_rows(g)
        near, far = by_1[row : row + n, :], by_3[row : row + n, :]
        high = jnp.where(tile < TILES - 1, jnp.where(even, near, far), 0.0)
        low = jnp.where(tile > 0, jnp.where(even, far, near), 0.0)
        edge = jnp.concatenate([high, jnp.zeros((8 - 2 * n, CZ), f32), low], 0)
        edges[g] = edge
        acc = columns(edge, g, lane, acc)
    for message in (z_even, z_odd):
        message[0:CY, :] = zpart[...]
        message[CY:LY, :] = acc


def outside_walls():
    tile = lax.axis_index("tile")
    row = lax.broadcasted_iota(jnp.int32, (LY, CZ), 0)
    return ((tile == 0) & (row == LY - 1)) | ((tile == TILES - 1) & (row == CY))


def flux(one, two, d):
    both = one[d] + two[d]
    return [0.25 * (one[i] + two[i]) * both for i in range(3)]


def advance(c, viscous, sides):
    spread = [0.0] * 3
    laplace = [0.0] * 3
    for d, (lower, upper) in enumerate(sides):
        f_up, f_down = flux(c, upper, d), flux(lower, c, d)
        spread = [spread[i] + (f_up[i] - f_down[i]) for i in range(3)]
        laplace = [laplace[i] + (upper[i] + lower[i]) for i in range(3)]
    return [
        c[i] + flow_step * (viscous * (laplace[i] - 6.0 * c[i]) - spread[i]) for i in range(3)
    ]


def both_ways(fields, step, axis):
    n = fields[0].shape[axis]
    return (
        [pltpu.roll(v, step, axis) for v in fields],
        [pltpu.roll(v, n - step, axis) for v in fields],
    )


def runge_kutta(near):
    def sample(e):
        weights = [(jnp.maximum(-v, 0.0), 1.0 - jnp.abs(v), jnp.maximum(v, 0.0)) for v in e]
        total = [0.0] * 3
        for dx in range(3):
            plane = [0.0] * 3
            for dy in range(3):
                for i in range(3):
                    line = sum(weights[2][dz] * near(i, dx, dy, dz) for dz in range(3))
                    plane[i] = plane[i] + weights[1][dy] * line
            total = [total[i] + weights[0][dx] * plane[i] for i in range(3)]
        return total

    k1 = [near(i, 1, 1, 1) for i in range(3)]
    k2 = sample([(0.5 * trace_step) * v for v in k1])
    k3 = sample([(0.5 * trace_step) * v for v in k2])
    k4 = sample([trace_step * v for v in k3])
    return [
        (trace_step / 6.0) * (k1[i] + 2.0 * k2[i] + 2.0 * k3[i] + k4[i]) for i in range(3)
    ]


def points_of(points, slot):
    s, r = divmod(slot, CAP)
    rows = points[s, 4 * r : 4 * r + 4, :].astype(jnp.int32)
    return [rows[k : k + 1] for k in range(4)]


def at_edge(z):
    return (z < 2) | (z >= CZ - 2)


def lanes_of(table, index):
    return jnp.take_along_axis(table, index, axis=1, mode="promise_in_bounds")


def main_kernel(
    own, early, late, odd, edges, by_3, by_1, by_2, mine, fresh, traced, strip, points, whole, near, table
):
    tile = lax.axis_index("tile")
    for s in range(TILES):
        part = jnp.where(tile == TILES - 1 - s, by_3[PT_ROW:ROWS, :], mine[...])
        part = jnp.where(tile == s + 1 - 2 * (s % 2), by_1[PT_ROW:ROWS, :], part)
        points[s] = jnp.where(tile == (s + 2) % TILES, by_2[...], part)
    lane = lax.broadcasted_iota(jnp.int32, (LY, CZ), 1)
    strips = [jnp.zeros((LY, CZ), f32) for _ in range(4)]
    for g in range(N_ALL):
        comp, x = group_of(g)
        whole[g, 0:CY, :] = plane_rows(g, 0, CY, own, early, late, odd)
        whole[g, CY:LY, :] = edges[g]
        plane = whole[g]
        place = WIDTH * x
        start_columns = pltpu.roll(plane, (place + 2) % CZ, 1)
        end_columns = pltpu.roll(plane, (place + 12) % CZ, 1)
        acc = jnp.where((lane >= place + 2) & (lane < place + 6), start_columns, strips[comp])
        strips[comp] = jnp.where((lane >= place + 8) & (lane < place + 12), end_columns, acc)
    for comp in range(4):
        strip[comp] = strips[comp]

    outside = outside_walls()
    for x in range(CX + 2):
        c = [whole[i * LX + x + 1] for i in range(3)]
        sides = [
            ([whole[i * LX + x] for i in range(3)], [whole[i * LX + x + 2] for i in range(3)]),
            both_ways(c, 1, 0),
            both_ways(c, 1, 1),
        ]
        new = advance(c, whole[N_VEL + x], sides)
        for i in range(3):
            if 1 <= x <= CX:
                fresh[i, x - 1] = new[i][:CY]
            a = jnp.where(outside, 0.0, new[i])
            for dz, field in enumerate((pltpu.roll(a, 1, 1), a, pltpu.roll(a, CZ - 1, 1))):
                near[x, i, 0, dz] = pltpu.roll(field, 1, 0)[:CY]
                near[x, i, 1, dz] = field[:CY]
                near[x, i, 2, dz] = pltpu.roll(field, LY - 1, 0)[:CY]

    for x in range(CX):
        moved = runge_kutta(lambda i, dx, dy, dz: near[x + dx, i, dy, dz])
        for i in range(3):
            table[i, x * CY : (x + 1) * CY, :] = moved[i]

    rows = lax.broadcasted_iota(jnp.int32, (CX * CY, CZ), 0)
    for slot in range(SLOTS):
        sx, sy, sz, steps = points_of(points, slot)
        here = (rows == sx * CY + sy) & (steps > 0) & ~at_edge(sz)
        index = jnp.broadcast_to(sz, (8, CZ))
        for i in range(3):
            got = jnp.concatenate(
                [lanes_of(table[i, 8 * k : 8 * k + 8, :], index) for k in range(CX * CY // 8)], 0
            )
            traced[i, slot : slot + 1, :] = jnp.sum(jnp.where(here, got, 0.0), 0, keepdims=True)


def strip_kernel(strip, early, late, odd, points, fresh_in, traced_in, fresh, traced):
    lane = lax.broadcasted_iota(jnp.int32, (LY, CZ), 1)
    place = lane % WIDTH
    even = is_even("sec")
    from_odd, from_even = odd[...], of_even_pair("sec", early[...], late[...], 2)
    low = jnp.where(even, from_odd, from_even)
    high = jnp.where(even, from_even, from_odd)
    fields = []
    for comp in range(4):
        before = pltpu.roll(low, (CZ - 4 * comp) % CZ, 1)
        after = pltpu.roll(high, (CZ + 10 - 4 * comp) % CZ, 1)
        own = strip[comp]
        own = jnp.where(place < 2, before, own)
        fields.append(jnp.where((place == 12) | (place == 13), after, own))
    c = fields[:3]
    new = advance(c, fields[3], [both_ways(c, WIDTH, 1), both_ways(c, 1, 0), both_ways(c, 1, 1)])

    column = lax.broadcasted_iota(jnp.int32, (CY, CZ), 1)
    for i in range(3):
        part = new[i][:CY]
        for x in range(CX):
            first = WIDTH * (x + 2)
            left = pltpu.roll(part, (CZ - first - 2) % CZ, 1)
            right = pltpu.roll(part, (2 * CZ - 1 - first - 11) % CZ, 1)
            value = jnp.where(column == CZ - 1, right, fresh_in[i, x])
            fresh[i, x] = jnp.where(column == 0, left, value)

    outside = outside_walls()
    near = {}
    for i in range(3):
        a = jnp.where(outside, 0.0, new[i])
        for dz, field in enumerate((pltpu.roll(a, 1, 1), a, pltpu.roll(a, CZ - 1, 1))):
            shifts = (pltpu.roll(field, 1, 0), field, pltpu.roll(field, LY - 1, 0))
            for dy, shifted in enumerate(shifts):
                part = shifted[:CY]
                near[i, 0, dy, dz] = pltpu.roll(part, WIDTH, 1)
                near[i, 1, dy, dz] = part
                near[i, 2, dy, dz] = pltpu.roll(part, CZ - WIDTH, 1)
    moved = runge_kutta(lambda *key: near[key])

    rows = lax.broadcasted_iota(jnp.int32, (CY, CZ), 0)
    for slot in range(SLOTS):
        sx, sy, sz, steps = points_of(points, slot)
        here = (rows == sy) & (steps > 0) & at_edge(sz)
        offset = jnp.where(sz < 2, sz + 2, sz - (CZ - 2) + 10)
        index = jnp.where(at_edge(sz), WIDTH * (sx + 2) + offset, 0)
        index = jnp.broadcast_to(index, (8, CZ))
        for i in range(3):
            got = jnp.concatenate([lanes_of(moved[i][8 * k : 8 * k + 8], index) for k in range(2)], 0)
            value = jnp.sum(jnp.where(here, got, 0.0), 0, keepdims=True)
            traced[i, slot : slot + 1, :] = traced_in[i, slot : slot + 1, :] + value


def shards(velocity, viscosity, counts, destination, seeds, substeps):
    def swap(value, axis, kept):
        n = lax.axis_size(axis)
        pairs = [(i, (i + 1) % n) for i in range(n) if kept(i)]
        return lax.ppermute(value, axis, pairs + [(b, a) for a, b in pairs])

    def swap_tiles(value, k):
        return lax.ppermute(value, "tile", [(i, i ^ k) for i in range(TILES)])

    def exchange(even, odd, axis, span=RUN // 2):
        early = swap(even, axis, lambda i: i % 2 == 0 and i % RUN < span)
        odd = swap(odd, axis, lambda i: i % 2 == 1)
        late = swap(even, axis, lambda i: i % 2 == 0 and i % RUN >= span)
        return early, late, odd

    message = shape(7, CY, CZ)
    own = jnp.concatenate([velocity.reshape(3 * CX, CY, CZ), viscosity], 0)
    x_odd, x_even = call(x_kernel, (message, message), [VMEM])(own)
    from_x = exchange(x_even, x_odd, "wide")
    base = call(
        points_kernel, shape(TILES, ROWS, CZ), [SMEM] + [VMEM] * 4, flops=1 << 20, moved=1 << 20
    )(
        destination.reshape(BLOCKS),
        counts,
        jnp.swapaxes(seeds.reshape(BLOCKS, 3, CZ), 0, 1),
        substeps.reshape(BLOCKS, CZ),
        own,
    )
    messages = (shape(ROWS, CZ), shape(ROWS, CZ), shape(ROWS - PT_ROW, CZ), shape(ROWS - PT_ROW, CZ))
    to_3, to_1, to_2, mine = call(
        y_kernel, messages, [VMEM] * 4, [pltpu.VMEM((TILES, ROWS, CZ), f32)]
    )(base, *from_x)
    by_3, by_1, by_2 = (
        swap_tiles(value, k) for value, k in ((to_3, 3), (to_1, 1), (to_2, 2))
    )
    zpart = call(z_kernel, shape(CY, CZ), [VMEM] * 4, flops=1 << 20, moved=1 << 20)(own, *from_x)
    edges, z_even, z_odd = call(
        edge_rows_kernel, (shape(N_ALL, 8, CZ), shape(LY, CZ), shape(LY, CZ)), [VMEM] * 3
    )(by_3, by_1, zpart)
    from_z = exchange(z_even, z_odd, "sec", 2)
    fresh, traced, strip, points = call(
        main_kernel,
        (
            shape(3, CX, CY, CZ),
            shape(3, SLOTS, CZ),
            shape(4, LY, CZ),
            shape(TILES, ROWS - PT_ROW, CZ),
        ),
        [VMEM] * 9,
        [
            pltpu.VMEM((N_ALL, LY, CZ), f32),
            pltpu.VMEM((CX + 2, 3, 3, 3, CY, CZ), f32),
            pltpu.VMEM((3, CX * CY, CZ), f32),
        ],
        flops=1 << 22,
        moved=1 << 23,
    )(own, *from_x, edges, by_3, by_1, by_2, mine)
    fresh, traced = call(
        strip_kernel, (shape(3, CX, CY, CZ), shape(3, SLOTS, CZ)), [VMEM] * 7
    )(strip, *from_z, points, fresh, traced)
    return fresh, jnp.swapaxes(traced, 0, 1)[None, None, None]


def solution(mesh):
    in_specs = (
        P(None, "wide", "tile", "sec"),
        P("wide", "tile", "sec"),
        P("wide", "sec", "tile"),
        P("wide", "sec", "tile", None),
        P("wide", "sec", "tile", None, None, None),
        P("wide", "sec", "tile", None, None),
    )
    out_specs = (P(None, "wide", "tile", "sec"), P("wide", "sec", "tile", None, None, None))

    return jax.shard_map(shards, mesh=mesh, in_specs=in_specs, out_specs=out_specs, check_vma=False)
```
